128 devices in a mesh: space: 16 (over z_lo, y, core), help: 8 (over z_hi, x).
Axes of the slice: x: 4, y: 4, z: 4 (z_hi: 2, z_lo: 2; z = z_hi * 2 + z_lo), core: 2. Of those that a mesh axis runs over, the one named last changes fastest.
Arguments:
- solution: float32 [9, 16384, 512], P(None, ('space', 'help')), may hold values from -6 to 6
- material: float32 [3, 16384, 512], P(None, ('space', 'help')), may hold values from 0.5 to 2
- neighbours: int32 [6, 16384], P(None, ('space', 'help')), may hold values from 0 to 16383, as said below
- refine_count: int32 [16, 8], P('space', 'help'), may hold values from 1 to 64, 256 in all within a row
Outputs:
- evolved: float32 [9, 16384, 512], P(None, ('space', 'help'))
The draws below stay inside these ranges and needn't reach their ends.
Inputs may be any that keep to these rules, and one draw needn't show every extreme that they name: The neighbours across y and z faces lie on the same device; across x+ on the device next along space (index + 1, wrapping) with the same help index, across x- on the previous one. Neighbours are mutual: the x+ neighbour's x- neighbour is the cell itself, likewise for y and z. `refine_count`: A device's cells whose index within the device is under its count are refined; the counts of one help group sum to 256.
All inputs are finite; a program needn't handle non-finite values.
Results may differ from the reference program's by a relative error of at most 0.0001.
Values sent between devices are 32-bit elements; how exact they have to be, the bound alone decides.
A program may use at most 128 MiB of HBM per device.

```python
import math
import jax
import jax.numpy as jnp
import numpy as np
from jax import lax

P_SIZE = 8
ORD = 8
ORD_LOW = 2
CELL_DEV = 128
OWNERS = 16
HELPERS = 8
NCELL = 16384
REF_MAX = 64
GROUP_REF = 256


def draw_neighbours(key, part):
    blocks = NCELL // CELL_DEV
    device_ids = jnp.arange(blocks, dtype=jnp.int32)

    def shuffled(salt):
        subkeys = jax.random.split(jax.random.fold_in(key, salt), blocks)
        return jax.vmap(lambda subkey: jax.random.permutation(subkey, CELL_DEV))(subkeys).astype(jnp.int32)
    forward = shuffled(11)
    across_y = shuffled(12)
    across_z = shuffled(13)
    later = (device_ids + HELPERS) % blocks
    earlier = (device_ids - HELPERS) % blocks
    backward = jnp.argsort(forward, axis=1, stable=True).astype(jnp.int32)
    offsets = device_ids[:, None] * CELL_DEV
    plus_x = later[:, None] * CELL_DEV + forward
    minus_x = earlier[:, None] * CELL_DEV + backward[earlier]
    plus_y = offsets + across_y
    minus_y = offsets + jnp.argsort(across_y, axis=1, stable=True).astype(jnp.int32)
    plus_z = offsets + across_z
    minus_z = offsets + jnp.argsort(across_z, axis=1, stable=True).astype(jnp.int32)
    linked = jnp.stack([minus_x, plus_x, minus_y, plus_y, minus_z, plus_z])
    return linked.reshape(6, NCELL).astype(jnp.int32)


def block_levels(stream_key, shape, cuts, smallest, top_value):
    gain = 1.0
    for position, blocks in cuts:
        heights = jax.random.uniform(jax.random.fold_in(jax.random.fold_in(stream_key, 6), position), (blocks,), jnp.float32, smallest / len(cuts), top_value / len(cuts))
        gain = gain * jnp.repeat(jnp.exp(heights), shape[position] // blocks).reshape((-1,) + (1,) * (len(shape) - 1 - position))
    return gain


def split_up(amount, total, limit, lean):
    portions = [(1 << 20) // math.isqrt(standing ** lean) + 1 for standing in range(2, amount + 1)]
    rest, given = total - limit - (amount - 1), [1] * (amount - 1)
    while rest > 0:
        candidates = [i for i in range(amount - 1) if given[i] < limit]
        whole, budget = sum([portions[i] for i in candidates]), rest
        for i in candidates:
            extra = min(limit - given[i], max(1, budget * portions[i] // whole), rest)
            given[i] = given[i] + extra
            rest = rest - extra
    return np.array([limit] + given)


def uneven(rng, count, total, limit, lean):
    if count == 2:
        one = jax.random.randint(rng, (), max(1, total - limit), min(limit, total - 1) + 1)
        return jnp.stack([one, total - one])
    tallies = jnp.asarray(split_up(count, total, limit, lean), jnp.int32)
    pairs = (count - 1) // 2
    donor, receiver = tallies[1:1 + 2 * pairs:2], tallies[2:2 + 2 * pairs:2]
    slack = jnp.minimum(donor - 1, limit - receiver)
    moved = jax.random.randint(jax.random.fold_in(rng, 1), (pairs,), 0, 1 << 20) % (slack + 1)
    tallies = tallies.at[1:1 + 2 * pairs:2].set(donor - moved).at[2:2 + 2 * pairs:2].set(receiver + moved)
    return tallies[jax.random.permutation(jax.random.fold_in(rng, 2), count)]


def noise(key, extent, spread, limit, cuts=(), kind=jnp.bfloat16):
    entries = spread * jax.random.normal(key, extent, jnp.float32)
    if cuts:
        entries = entries * block_levels(key, extent, cuts, -0.22, 0.18)
    return jnp.clip(entries, -limit, limit).astype(kind)


def setup_inputs(seed: int = 0) -> dict:
    seeds = jax.random.split(jax.random.key(seed), 5)
    solution = noise(seeds[0], (9, NCELL, P_SIZE * P_SIZE * P_SIZE), 1.0, 6.0, ((1, 128),), jnp.float32)
    material = jnp.clip(0.5 + 1.5 * jax.random.uniform(seeds[1], (3, NCELL, P_SIZE * P_SIZE * P_SIZE), jnp.float32) ** block_levels(seeds[1], (3, NCELL, P_SIZE * P_SIZE * P_SIZE), ((1, 128),), -0.2, 0.2), 0.5, 2.0)
    neighbours = draw_neighbours(jax.random.fold_in(seeds[4], 71), 0)
    refine_count = jax.vmap(lambda own: uneven(own, HELPERS, GROUP_REF, REF_MAX, 2))(jax.random.split(seeds[3], OWNERS)).reshape((OWNERS, HELPERS)).astype(jnp.int32)
    return {"solution": solution, "material": material, "neighbours": neighbours, "refine_count": refine_count}


along_x = (6, 7, 8, 0, 3, 5)
along_y = (6, 7, 8, 3, 1, 4)
along_z = (6, 7, 8, 5, 4, 2)
time_step = 0.5
lift_gain = 0.5

def cheb_table(node_count):
    intervals = node_count - 1
    places = np.arange(node_count)
    points = np.cos(np.pi * places / intervals)
    weights = np.where((places == 0) | (places == intervals), 2.0, 1.0)
    scaled = weights * (-1.0) ** places
    differ = points[:, None] - points[None, :] + np.eye(node_count)
    matrix = np.outer(scaled, 1.0 / scaled) / differ
    matrix = matrix - np.eye(node_count) * np.sum(matrix, axis=1)[:, None]
    return matrix / (node_count * node_count / 4.0)

def taylor_weight(degree):
    return time_step ** (degree + 1) / math.factorial(degree + 1)

def derive(values, slope_table, direction):
    fields, cell_count = (values.shape[0], values.shape[1])
    volume = values.reshape(fields, cell_count, P_SIZE, P_SIZE, P_SIZE)
    pattern = ('ij,vcjbe->vcibe', 'ij,vcaje->vcaie', 'ij,vcabj->vcabi')[direction]
    result = jnp.einsum(pattern, slope_table, volume, precision=lax.Precision.HIGHEST)
    return result.reshape(fields, cell_count, P_SIZE * P_SIZE * P_SIZE)

def elastic(slope_x, slope_y, slope_z, material):
    density, lame_first, shear_modulus = (material[0], material[1], material[2])
    diverge = slope_x[0] + slope_y[1] + slope_z[2]
    normal_x = lame_first * diverge + 2.0 * shear_modulus * slope_x[0]
    normal_y = lame_first * diverge + 2.0 * shear_modulus * slope_y[1]
    normal_z = lame_first * diverge + 2.0 * shear_modulus * slope_z[2]
    shear_xy = shear_modulus * (slope_y[0] + slope_x[1])
    shear_yz = shear_modulus * (slope_z[1] + slope_y[2])
    shear_xz = shear_modulus * (slope_z[0] + slope_x[2])
    speed_x = (slope_x[3] + slope_y[3] + slope_z[3]) / density
    speed_y = (slope_x[4] + slope_y[4] + slope_z[4]) / density
    speed_z = (slope_x[5] + slope_y[5] + slope_z[5]) / density
    return jnp.stack([normal_x, normal_y, normal_z, shear_xy, shear_yz, shear_xz, speed_x, speed_y, speed_z])

def operate(values, material, slope_table):
    picks = (along_x, along_y, along_z)
    slopes = [derive(jnp.stack([values[member] for member in picks[direction]]), slope_table, direction) for direction in range(3)]
    return elastic(slopes[0], slopes[1], slopes[2], material)

def face_trace(values, direction, place):
    fields, cell_count = (values.shape[0], values.shape[1])
    volume = values.reshape(fields, cell_count, P_SIZE, P_SIZE, P_SIZE)
    chosen = (slice(None), slice(None)) + (slice(None),) * direction + (place,)
    return volume[chosen].reshape(fields, cell_count, P_SIZE * P_SIZE)

def add_trace(volume, correction, direction, place):
    fields, cell_count = (volume.shape[0], volume.shape[1])
    chosen = (slice(None), slice(None)) + (slice(None),) * direction + (place,)
    return volume.at[chosen].add(correction.reshape(fields, cell_count, P_SIZE, P_SIZE))

def face_flux(own_trace, far_trace, own_speed, far_speed, medium, direction, normal_sign):
    picks = (along_x, along_y, along_z)
    difference = far_trace - own_trace
    top_speed = jnp.maximum(own_speed, far_speed)
    nothing = (0.0,) * 6
    slopes = [nothing, nothing, nothing]
    slopes[direction] = tuple((difference[member] for member in picks[direction]))
    normal = elastic(slopes[0], slopes[1], slopes[2], medium)
    return lift_gain * (0.5 * normal_sign * normal + 0.5 * top_speed[None] * difference)

def continue_terms(current, material, slope_table):
    extra_part = jnp.zeros_like(current)
    for degree in range(ORD_LOW, ORD):
        current = operate(current, material, slope_table)
        extra_part = extra_part + taylor_weight(degree) * current
    return extra_part

def predict(solution, material, slope_table):
    current = solution
    base_part = time_step * solution
    for degree in range(1, ORD_LOW):
        current = operate(current, material, slope_table)
        base_part = base_part + taylor_weight(degree) * current
    return (base_part, continue_terms(current, material, slope_table))

def reference(solution, material, neighbours, refine_count):
    slope_table = jnp.asarray(cheb_table(P_SIZE), jnp.float32)
    blocks = solution.shape[1] // CELL_DEV
    counts = refine_count.reshape(-1)
    local_ids = jnp.arange(CELL_DEV, dtype=jnp.int32)

    def predict_block(block_index, buffer):
        offset = (block_index * CELL_DEV).astype(jnp.int32)
        values = lax.dynamic_slice_in_dim(solution, offset, CELL_DEV, 1)
        medium = lax.dynamic_slice_in_dim(material, offset, CELL_DEV, 1)
        refined_limit = lax.dynamic_index_in_dim(counts, block_index.astype(jnp.int32), 0, keepdims=False)
        base_part, extra_part = predict(values, medium, slope_table)
        refined = local_ids < refined_limit
        combined = base_part + jnp.where(refined[None, :, None], extra_part, 0.0)
        return lax.dynamic_update_slice_in_dim(buffer, combined, offset, 1)
    integral = lax.fori_loop(0, blocks, predict_block, jnp.zeros_like(solution))
    wave_speed = jnp.sqrt((material[1] + 2.0 * material[2]) / material[0])

    def correct_block(block_index, buffer):
        offset = (block_index * CELL_DEV).astype(jnp.int32)
        values = lax.dynamic_slice_in_dim(integral, offset, CELL_DEV, 1)
        medium = lax.dynamic_slice_in_dim(material, offset, CELL_DEV, 1)
        start_state = lax.dynamic_slice_in_dim(solution, offset, CELL_DEV, 1)
        neighbour_ids = lax.dynamic_slice_in_dim(neighbours, offset, CELL_DEV, 1)
        speeds = lax.dynamic_slice_in_dim(wave_speed, offset, CELL_DEV, 0)
        result = start_state + operate(values, medium, slope_table)
        volume = result.reshape(9, CELL_DEV, P_SIZE, P_SIZE, P_SIZE)
        for face_id in range(6):
            direction = face_id // 2
            upper_side = face_id % 2 == 1
            own_place = 0 if upper_side else P_SIZE - 1
            far_place = P_SIZE - 1 if upper_side else 0
            normal_sign = 1.0 if upper_side else -1.0
            partner = jnp.take(integral, neighbour_ids[face_id], axis=1)
            partner_speed = jnp.take(wave_speed, neighbour_ids[face_id], axis=0)
            correction = face_flux(face_trace(values, direction, own_place), face_trace(partner, direction, far_place), face_trace(speeds[None], direction, own_place)[0], face_trace(partner_speed[None], direction, far_place)[0], face_trace(medium, direction, own_place), direction, normal_sign)
            volume = add_trace(volume, correction, direction, own_place)
        return lax.dynamic_update_slice_in_dim(buffer, volume.reshape(9, CELL_DEV, P_SIZE * P_SIZE * P_SIZE), offset, 1)
    return lax.fori_loop(0, blocks, correct_block, jnp.zeros_like(solution))
```

```python
import math

import jax
import jax.numpy as jnp
import ml_dtypes
import numpy as np
from jax import lax
from jax.experimental import pallas as pl
from jax.experimental.pallas import tpu as pltpu
from jax.sharding import PartitionSpec as P

ORD = 8
NODES = 512
PLANE = 64
CELLS = 128
STEP = 0.5
LIFT = 0.5
F32 = jnp.float32
BF16 = jnp.bfloat16
VMEM_LIMIT = 40 * 2**20

COLS = {6: 0, 7: 1, 8: 2, 4: 3, 3: 4, 1: 5, 5: 6, 2: 7}
X_FIELDS = (6, 7, 8, 0, 3, 5)


def cheb_table(node_count):
    intervals = node_count - 1
    places = np.arange(node_count)
    points = np.cos(np.pi * places / intervals)
    weights = np.where((places == 0) | (places == intervals), 2.0, 1.0)
    scaled = weights * (-1.0) ** places
    differ = points[:, None] - points[None, :] + np.eye(node_count)
    matrix = np.outer(scaled, 1.0 / scaled) / differ
    matrix = matrix - np.eye(node_count) * np.sum(matrix, axis=1)[:, None]
    return matrix / (node_count * node_count / 4.0)


TABLE = cheb_table(8)
EVEN = [[float((TABLE[i, j] + TABLE[i, 7 - j]) / 2) for j in range(4)] for i in range(4)]
ODD = [[float((TABLE[i, j] - TABLE[i, 7 - j]) / 2) for j in range(4)] for i in range(4)]


def plane_table():
    both = np.concatenate([np.kron(TABLE, np.eye(8)), np.kron(np.eye(8), TABLE)])
    both = both.astype(np.float32)
    high = both.astype(ml_dtypes.bfloat16)
    low = (both - high.astype(np.float32)).astype(ml_dtypes.bfloat16)
    return np.concatenate([high, high, low], axis=1)


def weight(degree):
    return STEP ** (degree + 1) / math.factorial(degree + 1)


def line_derivative(lines):
    plus = [lines[j] + lines[7 - j] for j in range(4)]
    minus = [lines[j] - lines[7 - j] for j in range(4)]
    out = [None] * 8
    for i in range(4):
        first = EVEN[i][0] * plus[0]
        second = ODD[i][0] * minus[0]
        for j in range(1, 4):
            first = first + EVEN[i][j] * plus[j]
            second = second + ODD[i][j] * minus[j]
        out[i] = second + first
        out[7 - i] = second - first
    return out


def rows(start, size):
    if isinstance(start, int):
        return pl.ds(start, size)
    return pl.ds(pl.multiple_of(start, 8), size)


def put_operand(r_ref, a, field, value):
    high = value.astype(BF16)
    low = (value - high.astype(F32)).astype(BF16)
    column = pl.ds(COLS[field] * CELLS, CELLS)
    base = a * 192
    if not isinstance(a, int):
        base = pl.multiple_of(base, 16)
    r_ref[pl.ds(base, 64), column] = high
    r_ref[pl.ds(base + 64, 64), column] = low
    r_ref[pl.ds(base + 128, 64), column] = high


def slopes(q_ref, r_ref, k_ref, t_ref, x_ref):
    def body(i, carry):
        base = pl.multiple_of(i * 192, 16)
        r = r_ref[pl.ds(base, 192), :]
        k = k_ref[...]
        both = jnp.dot(k, r[:, :512], preferred_element_type=F32)
        along_y = jnp.dot(k[:64], r[:, 512:768], preferred_element_type=F32)
        along_z = jnp.dot(k[64:], r[:, 768:], preferred_element_type=F32)

        def put(slot, value):
            t_ref[rows(slot * NODES + i * PLANE, PLANE), :] = value

        put(0, both[:64, 128:256])
        put(1, both[64:, 256:384])
        put(2, both[:64, :128])
        put(3, both[64:, 128:256] + both[:64, 256:384])
        put(4, both[64:, :128])
        put(5, along_y[:, :128] + along_z[:, :128])
        put(6, along_y[:, 128:] + both[64:, 384:])
        put(7, both[:64, 384:] + along_z[:, 128:])
        for slot, field in enumerate(X_FIELDS):
            lines = [q_ref[rows(field * NODES + a * PLANE + i * 8, 8), :] for a in range(8)]
            for a, value in enumerate(line_derivative(lines)):
                x_ref[rows(slot * NODES + a * PLANE + i * 8, 8), :] = value
        return carry

    lax.fori_loop(0, 8, body, 0)


def elastic_plane(a, t_ref, x_ref, m_ref):
    def t(slot):
        return t_ref[rows(slot * NODES + a * PLANE, PLANE), :]

    def x(slot):
        return x_ref[rows(slot * NODES + a * PLANE, PLANE), :]

    def m(slot):
        return m_ref[rows(slot * NODES + a * PLANE, PLANE), :]

    lam, shear, inverse = m(0), m(1), m(2)
    twice = shear + shear
    xx, yy, zz = x(0), t(0), t(1)
    spread = lam * (xx + yy + zz)
    return [
        spread + twice * xx,
        spread + twice * yy,
        spread + twice * zz,
        shear * (t(2) + x(1)),
        shear * t(3),
        shear * (t(4) + x(2)),
        inverse * (x(3) + t(5)),
        inverse * (x(4) + t(6)),
        inverse * (x(5) + t(7)),
    ]


def predict_kernel(
    sol_ref, mat_ref, count_ref, w_ref, k_ref,
    q0_ref, i_ref, m_ref, low_ref, high_ref, mface_ref,
    q_ref, r_ref, t_ref, x_ref,
):
    for field in range(9):
        for tile in range(4):
            block = sol_ref[field, :, tile * 128 : (tile + 1) * 128].T
            at = pl.ds(field * NODES + tile * 128, 128)
            q0_ref[at, :] = block
            q_ref[at, :] = block
            if field in COLS:
                put_operand(r_ref, 2 * tile, field, block[:64])
                put_operand(r_ref, 2 * tile + 1, field, block[64:])
    for tile in range(4):
        span = slice(tile * 128, (tile + 1) * 128)
        density = mat_ref[0, :, span].T
        lam = mat_ref[1, :, span].T
        shear = mat_ref[2, :, span].T
        inverse = 1.0 / density
        for slot, value in enumerate(
            (lam, shear, inverse, jnp.sqrt((lam + 2.0 * shear) / density))
        ):
            m_ref[pl.ds(slot * NODES + tile * 128, 128), :] = value

    slopes(q_ref, r_ref, k_ref, t_ref, x_ref)

    def first(a, carry):
        for field, value in enumerate(elastic_plane(a, t_ref, x_ref, m_ref)):
            at = rows(field * NODES + a * PLANE, PLANE)
            i_ref[at, :] = weight(0) * q0_ref[at, :] + weight(1) * value
            q_ref[at, :] = value
            if field in COLS:
                put_operand(r_ref, a, field, value)
        return carry

    lax.fori_loop(0, 8, first, 0)
    refined = lax.broadcasted_iota(jnp.int32, (8, CELLS), 1) < count_ref[0, 0]

    def term(degree, carry):
        slopes(q_ref, r_ref, k_ref, t_ref, x_ref)
        share = jnp.where(refined, w_ref[degree], 0.0)[None]

        def later(a, inner):
            for field, value in enumerate(elastic_plane(a, t_ref, x_ref, m_ref)):
                at = rows(field * NODES + a * PLANE, PLANE)
                added = (value.reshape(8, 8, CELLS) * share).reshape(PLANE, CELLS)
                i_ref[at, :] = i_ref[at, :] + added
                q_ref[at, :] = value
                if field in COLS:
                    put_operand(r_ref, a, field, value)
            return inner

        lax.fori_loop(0, 8, later, 0)
        return carry

    lax.fori_loop(2, ORD, term, 0)
    for out_ref, a in ((low_ref, 0), (high_ref, 7)):
        for field in range(9):
            out_ref[pl.ds(field * PLANE, PLANE), :] = i_ref[pl.ds(field * NODES + a * PLANE, PLANE), :]
        out_ref[pl.ds(9 * PLANE, PLANE), :] = m_ref[pl.ds(3 * NODES + a * PLANE, PLANE), :]
    for side, a in enumerate((0, 7)):
        for slot in range(3):
            mface_ref[pl.ds((side * 3 + slot) * PLANE, PLANE), :] = m_ref[
                pl.ds(slot * NODES + a * PLANE, PLANE), :
            ]


def fetch(far, targets):
    high = far.astype(BF16)
    low = (far - high.astype(F32)).astype(BF16)
    picks = (
        lax.broadcasted_iota(jnp.int32, (CELLS, CELLS), 0) == jnp.broadcast_to(targets, (CELLS, CELLS))
    ).astype(F32).astype(BF16)
    return jnp.dot(
        jnp.concatenate([high, low], axis=1),
        jnp.concatenate([picks, picks], axis=0),
        preferred_element_type=F32,
    )


def flux(own, far, lam, shear, inverse, direction, sign):
    jump = [far[f] - own[f] for f in range(9)]
    top = jnp.maximum(own[9], far[9]) * (0.5 * LIFT)
    scale = 0.5 * LIFT * sign
    lam, shear, inverse = lam * scale, shear * scale, inverse * scale
    normal = {0: 6, 1: 7, 2: 8}[direction]
    stress = {0: (0, 3, 5), 1: (3, 1, 4), 2: (5, 4, 2)}[direction]
    out = [top * jump[f] for f in range(9)]
    across = lam * jump[normal]
    for f in range(3):
        out[f] = out[f] + across
    out[direction] = out[direction] + 2.0 * shear * jump[normal]
    for other in range(3):
        if other != direction:
            slot = {(0, 1): 3, (1, 2): 4, (0, 2): 5}[(min(direction, other), max(direction, other))]
            out[slot] = out[slot] + shear * jump[6 + other]
    for other in range(3):
        out[6 + other] = out[6 + other] + inverse * jump[stress[other]]
    return out


def correct_kernel(i_ref, q0_ref, m_ref, n_ref, k_ref, e_ref, r_ref, t_ref, x_ref, far_ref):
    def split(a, carry):
        for field in COLS:
            put_operand(r_ref, a, field, i_ref[rows(field * NODES + a * PLANE, PLANE), :])
        return carry

    lax.fori_loop(0, 8, split, 0)
    slopes(i_ref, r_ref, k_ref, t_ref, x_ref)

    def volume(a, carry):
        for field, value in enumerate(elastic_plane(a, t_ref, x_ref, m_ref)):
            at = rows(field * NODES + a * PLANE, PLANE)
            e_ref[at, :] = q0_ref[at, :] + value
        return carry

    lax.fori_loop(0, 8, volume, 0)

    def y_face(ref, slot, place):
        return [ref[pl.ds(slot * NODES + a * PLANE + place * 8, 8), :] for a in range(8)]

    def z_face(ref, slot, place):
        return ref[pl.ds(slot * NODES + place, PLANE, stride=8), :]

    for face in (2, 3):
        own_place, far_place, sign = (0, 7, 1.0) if face % 2 else (7, 0, -1.0)
        targets = n_ref[pl.ds(face, 1), :] & (CELLS - 1)
        far = jnp.concatenate(
            [x for f in range(9) for x in y_face(i_ref, f, far_place)] + y_face(m_ref, 3, far_place), axis=0
        )
        far_ref[...] = fetch(far, targets)
        for a in range(8):
            at = a * PLANE + own_place * 8

            def pick(ref, slot):
                return ref[pl.ds(slot * NODES + at, 8), :]

            own = [pick(i_ref, f) for f in range(9)] + [pick(m_ref, 3)]
            other = [far_ref[pl.ds(f * PLANE + a * 8, 8), :] for f in range(10)]
            for f, value in enumerate(
                flux(own, other, pick(m_ref, 0), pick(m_ref, 1), pick(m_ref, 2), 1, sign)
            ):
                e_ref[pl.ds(f * NODES + at, 8), :] = pick(e_ref, f) + value
    for face in (4, 5):
        own_place, far_place, sign = (0, 7, 1.0) if face % 2 else (7, 0, -1.0)
        targets = n_ref[pl.ds(face, 1), :] & (CELLS - 1)
        far = jnp.concatenate(
            [z_face(i_ref, f, far_place) for f in range(9)] + [z_face(m_ref, 3, far_place)], axis=0
        )
        got = fetch(far, targets)
        own = [z_face(i_ref, f, own_place) for f in range(9)] + [z_face(m_ref, 3, own_place)]
        other = [got[f * PLANE : (f + 1) * PLANE] for f in range(10)]
        for f, value in enumerate(
            flux(own, other, z_face(m_ref, 0, own_place), z_face(m_ref, 1, own_place), z_face(m_ref, 2, own_place), 2, sign)
        ):
            e_ref[pl.ds(f * NODES + own_place, PLANE, stride=8), :] = z_face(e_ref, f, own_place) + value


def finish_kernel(e_ref, low_ref, high_ref, mface_ref, before_ref, after_ref, n_ref, out_ref, x_ref):
    for face, far_ref, own_ref, side, sign in ((0, before_ref, high_ref, 1, -1.0), (1, after_ref, low_ref, 0, 1.0)):
        got = fetch(far_ref[...], n_ref[pl.ds(face, 1), :] & (CELLS - 1))
        own = [own_ref[pl.ds(f * PLANE, PLANE), :] for f in range(10)]
        other = [got[f * PLANE : (f + 1) * PLANE] for f in range(10)]
        lam, shear, inverse = (mface_ref[pl.ds((side * 3 + s) * PLANE, PLANE), :] for s in range(3))
        for f, value in enumerate(flux(own, other, lam, shear, inverse, 0, sign)):
            x_ref[pl.ds((side * 9 + f) * PLANE, PLANE), :] = value
    for field in range(9):
        for tile in range(4):
            block = e_ref[pl.ds(field * NODES + tile * 128, 128), :]
            if tile == 0:
                block = jnp.concatenate([block[:64] + x_ref[pl.ds(field * PLANE, PLANE), :], block[64:]], axis=0)
            if tile == 3:
                block = jnp.concatenate(
                    [block[:64], block[64:] + x_ref[pl.ds((9 + field) * PLANE, PLANE), :]], axis=0
                )
            out_ref[field, :, tile * 128 : (tile + 1) * 128] = block.T


def shifted(value, axis, by):
    peers = lax.axis_size(axis)
    return lax.ppermute(value, axis, [(i, (i + by) % peers) for i in range(peers)])


def shape(*dims):
    return jax.ShapeDtypeStruct(dims, F32)


def whole():
    return pl.BlockSpec(memory_space=pltpu.VMEM)


def predict(solution, material, refine_count):
    table = jnp.asarray(plane_table())
    weights = jnp.asarray([weight(k) for k in range(ORD)], F32)
    smem = pl.BlockSpec(memory_space=pltpu.SMEM)
    return pl.pallas_call(
        predict_kernel,
        out_shape=(
            shape(9 * NODES, CELLS),
            shape(9 * NODES, CELLS),
            shape(4 * NODES, CELLS),
            shape(10 * PLANE, CELLS),
            shape(10 * PLANE, CELLS),
            shape(6 * PLANE, CELLS),
        ),
        in_specs=[whole(), whole(), smem, smem, whole()],
        out_specs=[whole()] * 6,
        scratch_shapes=[
            pltpu.VMEM((9 * NODES, CELLS), F32),
            pltpu.VMEM((8 * 192, 8 * CELLS), BF16),
            pltpu.VMEM((8 * NODES, CELLS), F32),
            pltpu.VMEM((6 * NODES, CELLS), F32),
        ],
        compiler_params=pltpu.CompilerParams(vmem_limit_bytes=VMEM_LIMIT),
        name="predict",
    )(solution, material, refine_count, weights, table)


def correct(integral, start, mats, neighbours):
    table = jnp.asarray(plane_table())
    return pl.pallas_call(
        correct_kernel,
        out_shape=shape(9 * NODES, CELLS),
        in_specs=[whole()] * 5,
        out_specs=whole(),
        scratch_shapes=[
            pltpu.VMEM((8 * 192, 8 * CELLS), BF16),
            pltpu.VMEM((8 * NODES, CELLS), F32),
            pltpu.VMEM((6 * NODES, CELLS), F32),
            pltpu.VMEM((10 * PLANE, CELLS), F32),
        ],
        compiler_params=pltpu.CompilerParams(vmem_limit_bytes=VMEM_LIMIT),
        cost_estimate=pl.CostEstimate(flops=8_000_000_000, bytes_accessed=30_000_000, transcendentals=0),
        name="correct",
    )(integral, start, mats, neighbours, table)


def finish(partial, low, high, mface, before, after, neighbours):
    return pl.pallas_call(
        finish_kernel,
        out_shape=shape(9, CELLS, NODES),
        in_specs=[whole()] * 7,
        out_specs=whole(),
        scratch_shapes=[pltpu.VMEM((18 * PLANE, CELLS), F32)],
        compiler_params=pltpu.CompilerParams(vmem_limit_bytes=VMEM_LIMIT),
        name="finish",
    )(partial, low, high, mface, before, after, neighbours)


def on_device(solution, material, neighbours, refine_count):
    start, integral, mats, low, high, mface = predict(solution, material, refine_count)
    after = shifted(high, "space", -1)
    before = shifted(low, "space", 1)
    partial = correct(integral, start, mats, neighbours)
    return finish(partial, low, high, mface, before, after, neighbours)


def solution(mesh):
    in_specs = (
        P(None, ("space", "help"), None),
        P(None, ("space", "help"), None),
        P(None, ("space", "help")),
        P("space", "help"),
    )
    out_specs = P(None, ("space", "help"), None)
    return jax.shard_map(
        on_device, mesh=mesh, in_specs=in_specs, out_specs=out_specs, check_vma=False
    )
```

```python
import math

import jax
import jax.numpy as jnp
import ml_dtypes
import numpy as np
from jax import lax
from jax.experimental import pallas as pl
from jax.experimental.pallas import tpu as pltpu
from jax.sharding import PartitionSpec as P

ORD = 8
NODES = 512
PLANE = 64
CELLS = 128
STEP = 0.5
LIFT = 0.5
F32 = jnp.float32
BF16 = jnp.bfloat16
VMEM_LIMIT = 40 * 2**20

COLS = (6, 7, 8, 4, 3, 1, 5, 2)
X_FIELDS = (6, 7, 8, 0, 3, 5)


def cheb_table(node_count):
    intervals = node_count - 1
    places = np.arange(node_count)
    points = np.cos(np.pi * places / intervals)
    weights = np.where((places == 0) | (places == intervals), 2.0, 1.0)
    scaled = weights * (-1.0) ** places
    differ = points[:, None] - points[None, :] + np.eye(node_count)
    matrix = np.outer(scaled, 1.0 / scaled) / differ
    matrix = matrix - np.eye(node_count) * np.sum(matrix, axis=1)[:, None]
    return matrix / (node_count * node_count / 4.0)


TABLE = cheb_table(8)
EVEN = [[float((TABLE[i, j] + TABLE[i, 7 - j]) / 2) for j in range(4)] for i in range(4)]
ODD = [[float((TABLE[i, j] - TABLE[i, 7 - j]) / 2) for j in range(4)] for i in range(4)]


def plane_table():
    both = np.concatenate([np.kron(TABLE, np.eye(8)), np.kron(np.eye(8), TABLE)])
    both = both.astype(np.float32)
    high = both.astype(ml_dtypes.bfloat16).astype(np.float32)
    low = (both - high).astype(ml_dtypes.bfloat16).astype(np.float32)
    return np.concatenate([high, high, low, np.zeros_like(low)], axis=1)


def weight(degree):
    return STEP ** (degree + 1) / math.factorial(degree + 1)


def line_derivative(lines):
    plus = [lines[j] + lines[7 - j] for j in range(4)]
    minus = [lines[j] - lines[7 - j] for j in range(4)]
    out = [None] * 8
    for i in range(4):
        first = EVEN[i][0] * plus[0]
        second = ODD[i][0] * minus[0]
        for j in range(1, 4):
            first = first + EVEN[i][j] * plus[j]
            second = second + ODD[i][j] * minus[j]
        out[i] = second + first
        out[7 - i] = second - first
    return out


def swap(value):
    return pltpu.roll(value, 64, axis=1)


def pair_derivative(lines, c_ref):
    sign = c_ref[pl.ds(128, 8), :]
    parts = [swap(v) + sign * v for v in lines]
    out = []
    for i in range(4):
        total = c_ref[pl.ds(i * 32, 8), :] * parts[0]
        for j in range(1, 4):
            total = total + c_ref[pl.ds(i * 32 + j * 8, 8), :] * parts[j]
        out.append(total + sign * swap(total))
    return out


def fill_pair_table(c_ref):
    lower = lax.broadcasted_iota(jnp.int32, (8, CELLS), 1) < 64
    for i in range(4):
        for j in range(4):
            c_ref[pl.ds(i * 32 + j * 8, 8), :] = jnp.where(lower, EVEN[i][j], ODD[i][j])
    c_ref[pl.ds(128, 8), :] = jnp.where(lower, 1.0, -1.0)


def plane(ref, slot, a, planes):
    return ref[pl.ds((slot * planes + a) * PLANE, PLANE), :]


def halves(value):
    high = value.astype(BF16)
    low = (value - high.astype(F32)).astype(BF16)
    return high, low


def slopes(q_ref, k_ref, t_ref, x_ref, planes, c_ref=None):
    k = k_ref[...].astype(BF16)[:, :192]

    def lines(b):
        for slot, field in enumerate(X_FIELDS):
            at = [pl.ds((field * planes + a) * PLANE + b * 8, 8) for a in range(planes)]
            values = [q_ref[place, :] for place in at]
            values = line_derivative(values) if c_ref is None else pair_derivative(values, c_ref)
            for a, value in enumerate(values):
                x_ref[pl.ds((slot * planes + a) * PLANE + b * 8, 8), :] = value

    for i in range(planes):
        split = {}
        for field in COLS:
            high, low = halves(plane(q_ref, field, i, planes))
            split[field] = jnp.concatenate([high, low, high], axis=0)

        def dot(left, fields):
            right = jnp.concatenate([split[f] for f in fields], axis=1)
            return jnp.dot(left, right, preferred_element_type=F32)

        both = dot(k, (6, 7, 8, 4))
        along_y = dot(k[:64], (3, 1))
        along_z = dot(k[64:], (5, 2))
        step = 8 // planes
        for b in range(i * step, (i + 1) * step):
            lines(b)

        def put(slot, value):
            t_ref[pl.ds((slot * planes + i) * PLANE, PLANE), :] = value

        put(0, both[:64, 128:256])
        put(1, both[64:, 256:384])
        put(2, both[:64, :128])
        put(3, both[64:, 128:256] + both[:64, 256:384])
        put(4, both[64:, :128])
        put(5, along_y[:, :128] + along_z[:, :128])
        put(6, along_y[:, 128:] + both[64:, 384:])
        put(7, both[:64, 384:] + along_z[:, 128:])


def elastic_plane(a, t_ref, x_ref, m_ref, planes, scale=None):
    def t(slot):
        return plane(t_ref, slot, a, planes)

    def x(slot):
        return plane(x_ref, slot, a, planes)

    lam, shear, inverse = (plane(m_ref, slot, a, planes) for slot in range(3))
    if scale is not None:
        lam, shear, inverse = lam * scale, shear * scale, inverse * scale
    twice = shear + shear
    xx, yy, zz = x(0), t(0), t(1)
    spread = lam * (xx + yy + zz)
    return [
        spread + twice * xx,
        spread + twice * yy,
        spread + twice * zz,
        shear * (t(2) + x(1)),
        shear * t(3),
        shear * (t(4) + x(2)),
        inverse * (x(3) + t(5)),
        inverse * (x(4) + t(6)),
        inverse * (x(5) + t(7)),
    ]


def predict_kernel(
    sol_hbm, mat_hbm, count_ref, k_hbm,
    q0_ref, i_ref, m_ref, low_ref, high_ref, mface_ref, k_ref,
    sol_ref, mat_ref, q_ref, u_ref, p_ref, t_ref, x_ref, c_ref, sem,
):
    copies = [pltpu.make_async_copy(sol_hbm.at[f], sol_ref.at[f], sem.at[f]) for f in range(9)]
    copies.append(pltpu.make_async_copy(mat_hbm, mat_ref, sem.at[9]))
    copies.append(pltpu.make_async_copy(k_hbm, k_ref, sem.at[10]))
    for copy in copies:
        copy.start()
    fill_pair_table(c_ref)
    for field in range(9):
        copies[field].wait()
        for tile in range(4):
            q0_ref[pl.ds(field * NODES + tile * 128, 128), :] = sol_ref[field, :, tile * 128 : (tile + 1) * 128].T
    copies[9].wait()
    copies[10].wait()
    for tile in range(4):
        span = slice(tile * 128, (tile + 1) * 128)
        density = mat_ref[0, :, span].T
        lam = mat_ref[1, :, span].T
        shear = mat_ref[2, :, span].T
        inverse = 1.0 / density
        for slot, value in enumerate(
            (lam, shear, inverse, jnp.sqrt((lam + 2.0 * shear) / density))
        ):
            m_ref[pl.ds(slot * NODES + tile * 128, 128), :] = value
    lower = lax.broadcasted_iota(jnp.int32, (PLANE, CELLS), 1) < 64

    def packed(first, second):
        return jnp.where(lower, first, swap(second))

    for slot in range(3):
        for j in range(4):
            p_ref[pl.ds((slot * 4 + j) * PLANE, PLANE), :] = packed(
                plane(m_ref, slot, j, 8), plane(m_ref, slot, 7 - j, 8)
            )

    slopes(q0_ref, k_ref, t_ref, x_ref, 8)
    for j in range(4):
        sides = [elastic_plane(a, t_ref, x_ref, m_ref, 8) for a in (j, 7 - j)]
        for field in range(9):
            for a, side in ((j, sides[0]), (7 - j, sides[1])):
                i_ref[pl.ds((field * 8 + a) * PLANE, PLANE), :] = (
                    weight(0) * plane(q0_ref, field, a, 8) + weight(1) * side[field]
                )
            value = packed(sides[0][field], sides[1][field])
            q_ref[pl.ds((field * 4 + j) * PLANE, PLANE), :] = value
            u_ref[pl.ds((field * 4 + j) * PLANE, PLANE), :] = value

    def nested(turn, scale):
        slopes(u_ref, k_ref, t_ref, x_ref, 4, c_ref)
        for j in range(4):
            for field, value in enumerate(elastic_plane(j, t_ref, x_ref, p_ref, 4, scale)):
                u_ref[pl.ds((field * 4 + j) * PLANE, PLANE), :] = plane(q_ref, field, j, 4) + value
        degree = (7 - turn).astype(F32)
        return scale * ((degree + 1.0) / degree)

    lax.fori_loop(0, ORD - 3, nested, jnp.float32(STEP / ORD))
    slopes(u_ref, k_ref, t_ref, x_ref, 4, c_ref)
    refined = lax.broadcasted_iota(jnp.int32, (PLANE, CELLS), 1) < count_ref[0, 0]
    for j in range(4):
        for field, value in enumerate(elastic_plane(j, t_ref, x_ref, p_ref, 4, weight(2))):
            for a, part in ((j, value), (7 - j, swap(value))):
                at = pl.ds((field * 8 + a) * PLANE, PLANE)
                i_ref[at, :] = i_ref[at, :] + jnp.where(refined, part, 0.0)

    for out_ref, a in ((low_ref, 0), (high_ref, 7)):
        for field in range(9):
            out_ref[pl.ds(field * PLANE, PLANE), :] = plane(i_ref, field, a, 8)
        out_ref[pl.ds(9 * PLANE, PLANE), :] = plane(m_ref, 3, a, 8)
    for side, a in enumerate((0, 7)):
        for slot in range(3):
            mface_ref[pl.ds((side * 3 + slot) * PLANE, PLANE), :] = plane(m_ref, slot, a, 8)


def fetch(far, targets):
    high = far.astype(BF16)
    low = (far - high.astype(F32)).astype(BF16)
    picks = (
        lax.broadcasted_iota(jnp.int32, (CELLS, CELLS), 0) == jnp.broadcast_to(targets, (CELLS, CELLS))
    ).astype(F32).astype(BF16)
    return jnp.dot(
        jnp.concatenate([high, low], axis=1),
        jnp.concatenate([picks, picks], axis=0),
        preferred_element_type=F32,
    )


def flux(own, far, lam, shear, inverse, direction, sign):
    jump = [far[f] - own[f] for f in range(9)]
    top = jnp.maximum(own[9], far[9]) * (0.5 * LIFT)
    scale = 0.5 * LIFT * sign
    lam, shear, inverse = lam * scale, shear * scale, inverse * scale
    normal = {0: 6, 1: 7, 2: 8}[direction]
    stress = {0: (0, 3, 5), 1: (3, 1, 4), 2: (5, 4, 2)}[direction]
    out = [top * jump[f] for f in range(9)]
    across = lam * jump[normal]
    for f in range(3):
        out[f] = out[f] + across
    out[direction] = out[direction] + 2.0 * shear * jump[normal]
    for other in range(3):
        if other != direction:
            slot = {(0, 1): 3, (1, 2): 4, (0, 2): 5}[(min(direction, other), max(direction, other))]
            out[slot] = out[slot] + shear * jump[6 + other]
    for other in range(3):
        out[6 + other] = out[6 + other] + inverse * jump[stress[other]]
    return out


def correct_kernel(i_ref, q0_ref, m_ref, n_ref, k_ref, e_ref, t_ref, x_ref, far_ref):
    slopes(i_ref, k_ref, t_ref, x_ref, 8)
    for a in range(8):
        for field, value in enumerate(elastic_plane(a, t_ref, x_ref, m_ref, 8)):
            at = pl.ds(field * NODES + a * PLANE, PLANE)
            e_ref[at, :] = q0_ref[at, :] + value

    def y_face(ref, slot, place):
        return [ref[pl.ds(slot * NODES + a * PLANE + place * 8, 8), :] for a in range(8)]

    def z_face(ref, slot, place):
        return ref[pl.ds(slot * NODES + place, PLANE, stride=8), :]

    for face in (2, 3):
        own_place, far_place, sign = (0, 7, 1.0) if face % 2 else (7, 0, -1.0)
        targets = n_ref[pl.ds(face, 1), :] & (CELLS - 1)
        far = jnp.concatenate(
            [x for f in range(9) for x in y_face(i_ref, f, far_place)] + y_face(m_ref, 3, far_place), axis=0
        )
        far_ref[...] = fetch(far, targets)
        for a in range(8):
            at = a * PLANE + own_place * 8

            def pick(ref, slot):
                return ref[pl.ds(slot * NODES + at, 8), :]

            own = [pick(i_ref, f) for f in range(9)] + [pick(m_ref, 3)]
            other = [far_ref[pl.ds(f * PLANE + a * 8, 8), :] for f in range(10)]
            for f, value in enumerate(
                flux(own, other, pick(m_ref, 0), pick(m_ref, 1), pick(m_ref, 2), 1, sign)
            ):
                e_ref[pl.ds(f * NODES + at, 8), :] = pick(e_ref, f) + value
    for face in (4, 5):
        own_place, far_place, sign = (0, 7, 1.0) if face % 2 else (7, 0, -1.0)
        targets = n_ref[pl.ds(face, 1), :] & (CELLS - 1)
        far = jnp.concatenate(
            [z_face(i_ref, f, far_place) for f in range(9)] + [z_face(m_ref, 3, far_place)], axis=0
        )
        got = fetch(far, targets)
        own = [z_face(i_ref, f, own_place) for f in range(9)] + [z_face(m_ref, 3, own_place)]
        other = [got[f * PLANE : (f + 1) * PLANE] for f in range(10)]
        for f, value in enumerate(
            flux(own, other, z_face(m_ref, 0, own_place), z_face(m_ref, 1, own_place), z_face(m_ref, 2, own_place), 2, sign)
        ):
            e_ref[pl.ds(f * NODES + own_place, PLANE, stride=8), :] = z_face(e_ref, f, own_place) + value


def finish_kernel(e_ref, low_ref, high_ref, mface_ref, before_ref, after_ref, n_ref, out_ref, x_ref):
    @pl.when(pl.program_id(0) == 0)
    def _():
        for face, far_ref, own_ref, side, sign in (
            (0, before_ref, high_ref, 1, -1.0),
            (1, after_ref, low_ref, 0, 1.0),
        ):
            got = fetch(far_ref[...], n_ref[pl.ds(face, 1), :] & (CELLS - 1))
            own = [own_ref[pl.ds(f * PLANE, PLANE), :] for f in range(10)]
            other = [got[f * PLANE : (f + 1) * PLANE] for f in range(10)]
            lam, shear, inverse = (mface_ref[pl.ds((side * 3 + s) * PLANE, PLANE), :] for s in range(3))
            for f, value in enumerate(flux(own, other, lam, shear, inverse, 0, sign)):
                x_ref[pl.ds((side * 9 + f) * PLANE, PLANE), :] = value

    base = pl.program_id(0) * 3
    for part in range(3):
        field = base + part
        for tile in range(4):
            block = e_ref[pl.ds(pl.multiple_of(field * NODES + tile * 128, 128), 128), :]
            low = x_ref[pl.ds(pl.multiple_of(field * PLANE, PLANE), PLANE), :]
            high = x_ref[pl.ds(pl.multiple_of((9 + field) * PLANE, PLANE), PLANE), :]
            if tile == 0:
                block = jnp.concatenate([block[:64] + low, block[64:]], axis=0)
            if tile == 3:
                block = jnp.concatenate([block[:64], block[64:] + high], axis=0)
            out_ref[part, :, tile * 128 : (tile + 1) * 128] = block.T


def shifted(value, axis, by):
    peers = lax.axis_size(axis)
    return lax.ppermute(value, axis, [(i, (i + by) % peers) for i in range(peers)])


def shape(*dims):
    return jax.ShapeDtypeStruct(dims, F32)


def whole():
    return pl.BlockSpec(memory_space=pltpu.VMEM)


def predict(solution, material, refine_count):
    table = jnp.asarray(plane_table())
    smem = pl.BlockSpec(memory_space=pltpu.SMEM)
    hbm = pl.BlockSpec(memory_space=pltpu.MemorySpace.HBM)
    return pl.pallas_call(
        predict_kernel,
        out_shape=(
            shape(9 * NODES, CELLS),
            shape(9 * NODES, CELLS),
            shape(4 * NODES, CELLS),
            shape(10 * PLANE, CELLS),
            shape(10 * PLANE, CELLS),
            shape(6 * PLANE, CELLS),
            shape(128, 256),
        ),
        in_specs=[hbm, hbm, smem, hbm],
        out_specs=[whole()] * 7,
        scratch_shapes=[
            pltpu.VMEM((9, CELLS, NODES), F32),
            pltpu.VMEM((3, CELLS, NODES), F32),
            pltpu.VMEM((9 * NODES // 2, CELLS), F32),
            pltpu.VMEM((9 * NODES // 2, CELLS), F32),
            pltpu.VMEM((3 * NODES // 2, CELLS), F32),
            pltpu.VMEM((8 * NODES, CELLS), F32),
            pltpu.VMEM((6 * NODES, CELLS), F32),
            pltpu.VMEM((136, CELLS), F32),
            pltpu.SemaphoreType.DMA((11,)),
        ],
        compiler_params=pltpu.CompilerParams(vmem_limit_bytes=VMEM_LIMIT),
        name="predict",
    )(solution, material, refine_count, table)


def correct(integral, start, mats, neighbours, table):
    return pl.pallas_call(
        correct_kernel,
        out_shape=shape(9 * NODES, CELLS),
        in_specs=[whole()] * 5,
        out_specs=whole(),
        scratch_shapes=[
            pltpu.VMEM((8 * NODES, CELLS), F32),
            pltpu.VMEM((6 * NODES, CELLS), F32),
            pltpu.VMEM((10 * PLANE, CELLS), F32),
        ],
        compiler_params=pltpu.CompilerParams(vmem_limit_bytes=VMEM_LIMIT),
        cost_estimate=pl.CostEstimate(flops=8_000_000_000, bytes_accessed=30_000_000, transcendentals=0),
        name="correct",
    )(integral, start, mats, neighbours, table)


def finish(partial, low, high, mface, before, after, neighbours):
    return pl.pallas_call(
        finish_kernel,
        out_shape=shape(9, CELLS, NODES),
        grid=(3,),
        in_specs=[whole()] * 7,
        out_specs=pl.BlockSpec((3, CELLS, NODES), lambda i: (i, 0, 0)),
        scratch_shapes=[pltpu.VMEM((18 * PLANE, CELLS), F32)],
        compiler_params=pltpu.CompilerParams(vmem_limit_bytes=VMEM_LIMIT),
        name="finish",
    )(partial, low, high, mface, before, after, neighbours)


def on_device(solution, material, neighbours, refine_count):
    start, integral, mats, low, high, mface, table = predict(solution, material, refine_count)
    after = shifted(high, "space", -1)
    before = shifted(low, "space", 1)
    partial = correct(integral, start, mats, neighbours, table)
    return finish(partial, low, high, mface, before, after, neighbours)


def solution(mesh):
    in_specs = (
        P(None, ("space", "help"), None),
        P(None, ("space", "help"), None),
        P(None, ("space", "help")),
        P("space", "help"),
    )
    out_specs = P(None, ("space", "help"), None)
    return jax.shard_map(
        on_device, mesh=mesh, in_specs=in_specs, out_specs=out_specs, check_vma=False
    )
```

```python
import math

import jax
import jax.numpy as jnp
import ml_dtypes
import numpy as np
from jax import lax
from jax.experimental import pallas as pl
from jax.experimental.pallas import tpu as pltpu
from jax.sharding import PartitionSpec as P

ORD = 8
NODES = 512
PLANE = 64
CELLS = 128
STEP = 0.5
LIFT = 0.5
F32 = jnp.float32
BF16 = jnp.bfloat16
VMEM_LIMIT = 61 * 2**20

COLS = (6, 7, 8, 4, 3, 1, 5, 2)
X_FIELDS = (6, 7, 8, 0, 3, 5)


def cheb_table(node_count):
    intervals = node_count - 1
    places = np.arange(node_count)
    points = np.cos(np.pi * places / intervals)
    weights = np.where((places == 0) | (places == intervals), 2.0, 1.0)
    scaled = weights * (-1.0) ** places
    differ = points[:, None] - points[None, :] + np.eye(node_count)
    matrix = np.outer(scaled, 1.0 / scaled) / differ
    matrix = matrix - np.eye(node_count) * np.sum(matrix, axis=1)[:, None]
    return matrix / (node_count * node_count / 4.0)


TABLE = cheb_table(8)
EVEN = [[float((TABLE[i, j] + TABLE[i, 7 - j]) / 2) for j in range(4)] for i in range(4)]
ODD = [[float((TABLE[i, j] - TABLE[i, 7 - j]) / 2) for j in range(4)] for i in range(4)]


def plane_table():
    both = np.concatenate([np.kron(TABLE, np.eye(8)), np.kron(np.eye(8), TABLE)])
    both = both.astype(np.float32)
    high = both.astype(ml_dtypes.bfloat16).astype(np.float32)
    low = (both - high).astype(ml_dtypes.bfloat16).astype(np.float32)
    return np.concatenate([high, high, low, np.zeros_like(low)], axis=1)


def weight(degree):
    return STEP ** (degree + 1) / math.factorial(degree + 1)


def line_derivative(lines):
    plus = [lines[j] + lines[7 - j] for j in range(4)]
    minus = [lines[j] - lines[7 - j] for j in range(4)]
    out = [None] * 8
    for i in range(4):
        first = EVEN[i][0] * plus[0]
        second = ODD[i][0] * minus[0]
        for j in range(1, 4):
            first = first + EVEN[i][j] * plus[j]
            second = second + ODD[i][j] * minus[j]
        out[i] = second + first
        out[7 - i] = second - first
    return out


def plane(ref, slot, a):
    return ref[pl.ds(slot * NODES + a * PLANE, PLANE), :]


def halves(value):
    high = value.astype(BF16)
    low = (value - high.astype(F32)).astype(BF16)
    return high, low


def slopes(q_ref, k_ref, t_ref, x_ref):
    k = k_ref[...].astype(BF16)[:, :192]

    for i in range(8):
        split = {}
        for field in COLS:
            high, low = halves(plane(q_ref, field, i))
            split[field] = jnp.concatenate([high, low, high], axis=0)

        def dot(left, fields):
            right = jnp.concatenate([split[f] for f in fields], axis=1)
            return jnp.dot(left, right, preferred_element_type=F32)

        both = dot(k, (6, 7, 8, 4))
        along_y = dot(k[:64], (3, 1))
        along_z = dot(k[64:], (5, 2))
        for slot, field in enumerate(X_FIELDS):
            lines = [q_ref[pl.ds(field * NODES + a * PLANE + i * 8, 8), :] for a in range(8)]
            for a, value in enumerate(line_derivative(lines)):
                x_ref[pl.ds(slot * NODES + a * PLANE + i * 8, 8), :] = value

        def put(slot, value):
            t_ref[pl.ds(slot * NODES + i * PLANE, PLANE), :] = value

        put(0, both[:64, 128:256])
        put(1, both[64:, 256:384])
        put(2, both[:64, :128])
        put(3, both[64:, 128:256] + both[:64, 256:384])
        put(4, both[64:, :128])
        put(5, along_y[:, :128] + along_z[:, :128])
        put(6, along_y[:, 128:] + both[64:, 384:])
        put(7, both[:64, 384:] + along_z[:, 128:])


def elastic_plane(a, t_ref, x_ref, m_ref, scale=None):
    def t(slot):
        return plane(t_ref, slot, a)

    def x(slot):
        return plane(x_ref, slot, a)

    lam, shear, inverse = (plane(m_ref, slot, a) for slot in range(3))
    if scale is not None:
        lam, shear, inverse = lam * scale, shear * scale, inverse * scale
    twice = shear + shear
    xx, yy, zz = x(0), t(0), t(1)
    spread = lam * (xx + yy + zz)
    return [
        spread + twice * xx,
        spread + twice * yy,
        spread + twice * zz,
        shear * (t(2) + x(1)),
        shear * t(3),
        shear * (t(4) + x(2)),
        inverse * (x(3) + t(5)),
        inverse * (x(4) + t(6)),
        inverse * (x(5) + t(7)),
    ]


def remote(src, dst, send, recv, peer):
    return pltpu.make_async_remote_copy(
        src_ref=src,
        dst_ref=dst,
        send_sem=send,
        recv_sem=recv,
        device_id={"space": peer},
        device_id_type=pl.DeviceIdType.MESH,
    )


def step_kernel(
    sol_hbm, mat_hbm, n_hbm, count_ref, k_hbm,
    e_hbm,
    sol_ref, mat_ref, n_ref, k_ref, q0_ref, q_ref, u_ref, i_ref, m_ref, t_ref, x_ref, far_ref,
    e_ref, before_ref, after_ref, low_ref, high_ref,
    sem, send_sem, recv_sem, out_sem,
):
    me = lax.axis_index("space")
    peers = lax.axis_size("space")
    right, left = lax.rem(me + 1, peers), lax.rem(me + peers - 1, peers)
    barrier = pltpu.get_barrier_semaphore()
    for peer in (left, right):
        pl.semaphore_signal(barrier, inc=1, device_id={"space": peer}, device_id_type=pl.DeviceIdType.MESH)

    copies = [pltpu.make_async_copy(sol_hbm.at[f], sol_ref.at[f], sem.at[f]) for f in range(9)]
    copies.append(pltpu.make_async_copy(mat_hbm, mat_ref, sem.at[9]))
    copies.append(pltpu.make_async_copy(k_hbm, k_ref, sem.at[10]))
    copies.append(pltpu.make_async_copy(n_hbm, n_ref, sem.at[11]))
    for copy in copies:
        copy.start()
    for field in range(9):
        copies[field].wait()
        for tile in range(4):
            q0_ref[pl.ds(field * NODES + tile * 128, 128), :] = sol_ref[field, :, tile * 128 : (tile + 1) * 128].T
    for copy in copies[9:]:
        copy.wait()
    for tile in range(4):
        span = slice(tile * 128, (tile + 1) * 128)
        density = mat_ref[0, :, span].T
        lam = mat_ref[1, :, span].T
        shear = mat_ref[2, :, span].T
        inverse = 1.0 / density
        for slot, value in enumerate(
            (lam, shear, inverse, jnp.sqrt((lam + 2.0 * shear) / density))
        ):
            m_ref[pl.ds(slot * NODES + tile * 128, 128), :] = value

    slopes(q0_ref, k_ref, t_ref, x_ref)
    for a in range(8):
        for field, value in enumerate(elastic_plane(a, t_ref, x_ref, m_ref)):
            at = pl.ds(field * NODES + a * PLANE, PLANE)
            i_ref[at, :] = weight(0) * plane(q0_ref, field, a) + weight(1) * value
            q_ref[at, :] = value
            u_ref[at, :] = value

    def nested(turn, scale):
        slopes(u_ref, k_ref, t_ref, x_ref)
        for a in range(8):
            for field, value in enumerate(elastic_plane(a, t_ref, x_ref, m_ref, scale)):
                u_ref[pl.ds(field * NODES + a * PLANE, PLANE), :] = plane(q_ref, field, a) + value
        degree = (7 - turn).astype(F32)
        return scale * ((degree + 1.0) / degree)

    lax.fori_loop(0, ORD - 3, nested, jnp.float32(STEP / ORD))
    slopes(u_ref, k_ref, t_ref, x_ref)
    refined = lax.broadcasted_iota(jnp.int32, (PLANE, CELLS), 1) < count_ref[0, 0]
    for a in range(8):
        for field, value in enumerate(elastic_plane(a, t_ref, x_ref, m_ref, weight(2))):
            at = pl.ds(field * NODES + a * PLANE, PLANE)
            i_ref[at, :] = i_ref[at, :] + jnp.where(refined, value, 0.0)

    for out_ref, a in ((low_ref, 0), (high_ref, 7)):
        for field in range(9):
            out_ref[pl.ds(field * PLANE, PLANE), :] = plane(i_ref, field, a)
        out_ref[pl.ds(9 * PLANE, PLANE), :] = plane(m_ref, 3, a)
    pl.semaphore_wait(barrier, 2)
    sends = [
        remote(low_ref, before_ref, send_sem.at[0], recv_sem.at[0], right),
        remote(high_ref, after_ref, send_sem.at[1], recv_sem.at[1], left),
    ]
    for send in sends:
        send.start()
    volume_and_faces(i_ref, q0_ref, m_ref, n_ref, k_ref, e_ref, t_ref, x_ref, far_ref)

    def writing(field, a, planes, slot):
        at = pl.ds(field * NODES + a * PLANE, planes * PLANE)
        return pltpu.make_async_copy(e_ref.at[at], e_hbm.at[at], out_sem.at[slot * 9 + field])

    writes = [writing(field, 1, 6, 0) for field in range(9)]
    for write in writes:
        write.start()
    for send in sends:
        send.wait()
    for face, far_ref, a, sign in ((0, before_ref, 7, -1.0), (1, after_ref, 0, 1.0)):
        got = fetch(far_ref[...], n_ref[pl.ds(face, 1), :] & (CELLS - 1))
        own = [plane(i_ref, f, a) for f in range(9)] + [plane(m_ref, 3, a)]
        other = [got[f * PLANE : (f + 1) * PLANE] for f in range(10)]
        lam, shear, inverse = (plane(m_ref, slot, a) for slot in range(3))
        for f, value in enumerate(flux(own, other, lam, shear, inverse, 0, sign)):
            e_ref[pl.ds(f * NODES + a * PLANE, PLANE), :] = plane(e_ref, f, a) + value
        for field in range(9):
            writes.append(writing(field, a, 1, 1 + face))
            writes[-1].start()
    for write in writes:
        write.wait()


def fetch(far, targets):
    high = far.astype(BF16)
    low = (far - high.astype(F32)).astype(BF16)
    picks = (
        lax.broadcasted_iota(jnp.int32, (CELLS, CELLS), 0) == jnp.broadcast_to(targets, (CELLS, CELLS))
    ).astype(F32).astype(BF16)
    return jnp.dot(
        jnp.concatenate([high, low], axis=1),
        jnp.concatenate([picks, picks], axis=0),
        preferred_element_type=F32,
    )


def flux(own, far, lam, shear, inverse, direction, sign):
    jump = [far[f] - own[f] for f in range(9)]
    top = jnp.maximum(own[9], far[9]) * (0.5 * LIFT)
    scale = 0.5 * LIFT * sign
    lam, shear, inverse = lam * scale, shear * scale, inverse * scale
    normal = {0: 6, 1: 7, 2: 8}[direction]
    stress = {0: (0, 3, 5), 1: (3, 1, 4), 2: (5, 4, 2)}[direction]
    out = [top * jump[f] for f in range(9)]
    across = lam * jump[normal]
    for f in range(3):
        out[f] = out[f] + across
    out[direction] = out[direction] + 2.0 * shear * jump[normal]
    for other in range(3):
        if other != direction:
            slot = {(0, 1): 3, (1, 2): 4, (0, 2): 5}[(min(direction, other), max(direction, other))]
            out[slot] = out[slot] + shear * jump[6 + other]
    for other in range(3):
        out[6 + other] = out[6 + other] + inverse * jump[stress[other]]
    return out


def volume_and_faces(i_ref, q0_ref, m_ref, n_ref, k_ref, e_ref, t_ref, x_ref, far_ref):
    slopes(i_ref, k_ref, t_ref, x_ref)
    for a in range(8):
        for field, value in enumerate(elastic_plane(a, t_ref, x_ref, m_ref)):
            at = pl.ds(field * NODES + a * PLANE, PLANE)
            e_ref[at, :] = q0_ref[at, :] + value

    def y_face(ref, slot, place):
        return [ref[pl.ds(slot * NODES + a * PLANE + place * 8, 8), :] for a in range(8)]

    def z_face(ref, slot, place):
        return ref[pl.ds(slot * NODES + place, PLANE, stride=8), :]

    for face in (2, 3):
        own_place, far_place, sign = (0, 7, 1.0) if face % 2 else (7, 0, -1.0)
        targets = n_ref[pl.ds(face, 1), :] & (CELLS - 1)
        far = jnp.concatenate(
            [x for f in range(9) for x in y_face(i_ref, f, far_place)] + y_face(m_ref, 3, far_place), axis=0
        )
        far_ref[...] = fetch(far, targets)
        for a in range(8):
            at = a * PLANE + own_place * 8

            def pick(ref, slot):
                return ref[pl.ds(slot * NODES + at, 8), :]

            own = [pick(i_ref, f) for f in range(9)] + [pick(m_ref, 3)]
            other = [far_ref[pl.ds(f * PLANE + a * 8, 8), :] for f in range(10)]
            for f, value in enumerate(
                flux(own, other, pick(m_ref, 0), pick(m_ref, 1), pick(m_ref, 2), 1, sign)
            ):
                e_ref[pl.ds(f * NODES + at, 8), :] = pick(e_ref, f) + value
    for face in (4, 5):
        own_place, far_place, sign = (0, 7, 1.0) if face % 2 else (7, 0, -1.0)
        targets = n_ref[pl.ds(face, 1), :] & (CELLS - 1)
        far = jnp.concatenate(
            [z_face(i_ref, f, far_place) for f in range(9)] + [z_face(m_ref, 3, far_place)], axis=0
        )
        got = fetch(far, targets)
        own = [z_face(i_ref, f, own_place) for f in range(9)] + [z_face(m_ref, 3, own_place)]
        other = [got[f * PLANE : (f + 1) * PLANE] for f in range(10)]
        for f, value in enumerate(
            flux(own, other, z_face(m_ref, 0, own_place), z_face(m_ref, 1, own_place), z_face(m_ref, 2, own_place), 2, sign)
        ):
            e_ref[pl.ds(f * NODES + own_place, PLANE, stride=8), :] = z_face(e_ref, f, own_place) + value


def finish_kernel(e_ref, out_ref):
    for tile in range(4):
        out_ref[0, :, tile * 128 : (tile + 1) * 128] = e_ref[tile * 128 : (tile + 1) * 128, :].T


def shape(*dims):
    return jax.ShapeDtypeStruct(dims, F32)


def step(solution, material, neighbours, refine_count):
    table = jnp.asarray(plane_table())
    smem = pl.BlockSpec(memory_space=pltpu.SMEM)
    hbm = pl.BlockSpec(memory_space=pltpu.MemorySpace.HBM)

    def field_buffer(count):
        return pltpu.VMEM((count * NODES, CELLS), F32)

    return pl.pallas_call(
        step_kernel,
        out_shape=shape(9 * NODES, CELLS),
        in_specs=[hbm, hbm, hbm, smem, hbm],
        out_specs=hbm,
        scratch_shapes=[
            pltpu.VMEM((9, CELLS, NODES), F32),
            pltpu.VMEM((3, CELLS, NODES), F32),
            pltpu.VMEM((6, CELLS), jnp.int32),
            pltpu.VMEM((128, 256), F32),
            field_buffer(9),
            field_buffer(9),
            field_buffer(9),
            field_buffer(9),
            field_buffer(4),
            field_buffer(8),
            field_buffer(6),
            pltpu.VMEM((10 * PLANE, CELLS), F32),
            field_buffer(9),
            pltpu.VMEM((10 * PLANE, CELLS), F32),
            pltpu.VMEM((10 * PLANE, CELLS), F32),
            pltpu.VMEM((10 * PLANE, CELLS), F32),
            pltpu.VMEM((10 * PLANE, CELLS), F32),
            pltpu.SemaphoreType.DMA((12,)),
            pltpu.SemaphoreType.DMA((2,)),
            pltpu.SemaphoreType.DMA((2,)),
            pltpu.SemaphoreType.DMA((27,)),
        ],
        compiler_params=pltpu.CompilerParams(
            vmem_limit_bytes=VMEM_LIMIT, collective_id=0, has_side_effects=True
        ),
        name="step",
    )(solution, material, neighbours, refine_count, table)


def finish(nodal):
    return pl.pallas_call(
        finish_kernel,
        out_shape=shape(9, CELLS, NODES),
        grid=(9,),
        in_specs=[pl.BlockSpec((NODES, CELLS), lambda i: (i, 0))],
        out_specs=pl.BlockSpec((1, CELLS, NODES), lambda i: (i, 0, 0)),
        compiler_params=pltpu.CompilerParams(vmem_limit_bytes=VMEM_LIMIT),
        name="finish",
    )(nodal)


def on_device(solution, material, neighbours, refine_count):
    return finish(step(solution, material, neighbours, refine_count))


def solution(mesh):
    in_specs = (
        P(None, ("space", "help"), None),
        P(None, ("space", "help"), None),
        P(None, ("space", "help")),
        P("space", "help"),
    )
    out_specs = P(None, ("space", "help"), None)
    return jax.shard_map(
        on_device, mesh=mesh, in_specs=in_specs, out_specs=out_specs, check_vma=False
    )
```

```python
import math

import jax
import jax.numpy as jnp
import ml_dtypes
import numpy as np
from jax import lax
from jax.experimental import pallas as pl
from jax.experimental.pallas import tpu as pltpu
from jax.sharding import PartitionSpec as P

ORD = 8
NODES = 512
PLANE = 64
CELLS = 128
STEP = 0.5
LIFT = 0.5
F32 = jnp.float32
BF16 = jnp.bfloat16
VMEM_LIMIT = 32 * 2**20

COLS = (6, 7, 8, 4, 3, 1, 5, 2)
X_FIELDS = (6, 7, 8, 0, 3, 5)


def cheb_table(node_count):
    intervals = node_count - 1
    places = np.arange(node_count)
    points = np.cos(np.pi * places / intervals)
    weights = np.where((places == 0) | (places == intervals), 2.0, 1.0)
    scaled = weights * (-1.0) ** places
    differ = points[:, None] - points[None, :] + np.eye(node_count)
    matrix = np.outer(scaled, 1.0 / scaled) / differ
    matrix = matrix - np.eye(node_count) * np.sum(matrix, axis=1)[:, None]
    return matrix / (node_count * node_count / 4.0)


TABLE = cheb_table(8)
EVEN = [[float((TABLE[i, j] + TABLE[i, 7 - j]) / 2) for j in range(4)] for i in range(4)]
ODD = [[float((TABLE[i, j] - TABLE[i, 7 - j]) / 2) for j in range(4)] for i in range(4)]


def plane_table():
    both = np.concatenate([np.kron(TABLE, np.eye(8)), np.kron(np.eye(8), TABLE)])
    both = both.astype(np.float32)
    high = both.astype(ml_dtypes.bfloat16).astype(np.float32)
    low = (both - high).astype(ml_dtypes.bfloat16).astype(np.float32)
    return np.concatenate([high, high, low, np.zeros_like(low)], axis=1)


def weight(degree):
    return STEP ** (degree + 1) / math.factorial(degree + 1)


def line_derivative(lines):
    plus = [lines[j] + lines[7 - j] for j in range(4)]
    minus = [lines[j] - lines[7 - j] for j in range(4)]
    out = [None] * 8
    for i in range(4):
        first = EVEN[i][0] * plus[0]
        second = ODD[i][0] * minus[0]
        for j in range(1, 4):
            first = first + EVEN[i][j] * plus[j]
            second = second + ODD[i][j] * minus[j]
        out[i] = second + first
        out[7 - i] = second - first
    return out


def plane(ref, slot, a):
    return ref[pl.ds(slot * NODES + a * PLANE, PLANE), :]


def halves(value):
    high = value.astype(BF16)
    low = (value - high.astype(F32)).astype(BF16)
    return high, low


def slopes(q_ref, k_ref, t_ref, x_ref):
    k = k_ref[...].astype(BF16)[:, :192]

    for i in range(8):
        split = {}
        for field in COLS:
            high, low = halves(plane(q_ref, field, i))
            split[field] = jnp.concatenate([high, low, high], axis=0)

        def dot(left, fields):
            right = jnp.concatenate([split[f] for f in fields], axis=1)
            return jnp.dot(left, right, preferred_element_type=F32)

        both = dot(k, (6, 7, 8, 4))
        along_y = dot(k[:64], (3, 1))
        along_z = dot(k[64:], (5, 2))
        for slot, field in enumerate(X_FIELDS):
            lines = [q_ref[pl.ds(field * NODES + a * PLANE + i * 8, 8), :] for a in range(8)]
            for a, value in enumerate(line_derivative(lines)):
                x_ref[pl.ds(slot * NODES + a * PLANE + i * 8, 8), :] = value

        def put(slot, value):
            t_ref[pl.ds(slot * NODES + i * PLANE, PLANE), :] = value

        put(0, both[:64, 128:256])
        put(1, both[64:, 256:384])
        put(2, both[:64, :128])
        put(3, both[64:, 128:256] + both[:64, 256:384])
        put(4, both[64:, :128])
        put(5, along_y[:, :128] + along_z[:, :128])
        put(6, along_y[:, 128:] + both[64:, 384:])
        put(7, both[:64, 384:] + along_z[:, 128:])


def elastic_plane(a, t_ref, x_ref, m_ref, scale=None):
    def t(slot):
        return plane(t_ref, slot, a)

    def x(slot):
        return plane(x_ref, slot, a)

    lam, shear, inverse = (plane(m_ref, slot, a) for slot in range(3))
    if scale is not None:
        lam, shear, inverse = lam * scale, shear * scale, inverse * scale
    twice = shear + shear
    xx, yy, zz = x(0), t(0), t(1)
    spread = lam * (xx + yy + zz)
    return [
        spread + twice * xx,
        spread + twice * yy,
        spread + twice * zz,
        shear * (t(2) + x(1)),
        shear * t(3),
        shear * (t(4) + x(2)),
        inverse * (x(3) + t(5)),
        inverse * (x(4) + t(6)),
        inverse * (x(5) + t(7)),
    ]


def remote(src, dst, send, recv, peer):
    return pltpu.make_async_remote_copy(
        src_ref=src,
        dst_ref=dst,
        send_sem=send,
        recv_sem=recv,
        device_id={"space": peer},
        device_id_type=pl.DeviceIdType.MESH,
    )


def step_kernel(
    sol_hbm, mat_hbm, n_hbm, count_ref, k_hbm,
    e_ref,
    sol_ref, mat_ref, n_ref, k_ref, q0_ref, q_ref, u_ref, i_ref, m_ref, t_ref, x_ref, far_ref,
    before_ref, after_ref, low_ref, high_ref,
    sem, send_sem, recv_sem,
):
    me = lax.axis_index("space")
    peers = lax.axis_size("space")
    right, left = lax.rem(me + 1, peers), lax.rem(me + peers - 1, peers)
    barrier = pltpu.get_barrier_semaphore()
    for peer in (left, right):
        pl.semaphore_signal(barrier, inc=1, device_id={"space": peer}, device_id_type=pl.DeviceIdType.MESH)

    copies = [pltpu.make_async_copy(sol_hbm.at[f], sol_ref.at[f], sem.at[f]) for f in range(9)]
    copies.append(pltpu.make_async_copy(mat_hbm, mat_ref, sem.at[9]))
    copies.append(pltpu.make_async_copy(k_hbm, k_ref, sem.at[10]))
    copies.append(pltpu.make_async_copy(n_hbm, n_ref, sem.at[11]))
    for copy in copies:
        copy.start()
    for field in range(9):
        copies[field].wait()
        for tile in range(4):
            q0_ref[pl.ds(field * NODES + tile * 128, 128), :] = sol_ref[field, :, tile * 128 : (tile + 1) * 128].T
    for copy in copies[9:]:
        copy.wait()
    for tile in range(4):
        span = slice(tile * 128, (tile + 1) * 128)
        density = mat_ref[0, :, span].T
        lam = mat_ref[1, :, span].T
        shear = mat_ref[2, :, span].T
        inverse = 1.0 / density
        for slot, value in enumerate(
            (lam, shear, inverse, jnp.sqrt((lam + 2.0 * shear) / density))
        ):
            m_ref[pl.ds(slot * NODES + tile * 128, 128), :] = value

    slopes(q0_ref, k_ref, t_ref, x_ref)
    for a in range(8):
        for field, value in enumerate(elastic_plane(a, t_ref, x_ref, m_ref)):
            at = pl.ds(field * NODES + a * PLANE, PLANE)
            i_ref[at, :] = weight(0) * plane(q0_ref, field, a) + weight(1) * value
            q_ref[at, :] = value
            u_ref[at, :] = value

    def nested(turn, scale):
        slopes(u_ref, k_ref, t_ref, x_ref)
        for a in range(8):
            for field, value in enumerate(elastic_plane(a, t_ref, x_ref, m_ref, scale)):
                u_ref[pl.ds(field * NODES + a * PLANE, PLANE), :] = plane(q_ref, field, a) + value
        degree = (7 - turn).astype(F32)
        return scale * ((degree + 1.0) / degree)

    lax.fori_loop(0, ORD - 3, nested, jnp.float32(STEP / ORD))
    slopes(u_ref, k_ref, t_ref, x_ref)
    refined = lax.broadcasted_iota(jnp.int32, (PLANE, CELLS), 1) < count_ref[0, 0]
    for a in range(8):
        for field, value in enumerate(elastic_plane(a, t_ref, x_ref, m_ref, weight(2))):
            at = pl.ds(field * NODES + a * PLANE, PLANE)
            i_ref[at, :] = i_ref[at, :] + jnp.where(refined, value, 0.0)

    for out_ref, a in ((low_ref, 0), (high_ref, 7)):
        for field in range(9):
            out_ref[pl.ds(field * PLANE, PLANE), :] = plane(i_ref, field, a)
        out_ref[pl.ds(9 * PLANE, PLANE), :] = plane(m_ref, 3, a)
    pl.semaphore_wait(barrier, 2)
    sends = [
        remote(low_ref, before_ref, send_sem.at[0], recv_sem.at[0], right),
        remote(high_ref, after_ref, send_sem.at[1], recv_sem.at[1], left),
    ]
    for send in sends:
        send.start()
    volume_and_faces(i_ref, q0_ref, m_ref, n_ref, k_ref, e_ref, t_ref, x_ref, far_ref)

    for send in sends:
        send.wait()
    for face, far_ref, a, sign in ((0, before_ref, 7, -1.0), (1, after_ref, 0, 1.0)):
        got = fetch(far_ref[...], n_ref[pl.ds(face, 1), :] & (CELLS - 1))
        own = [plane(i_ref, f, a) for f in range(9)] + [plane(m_ref, 3, a)]
        other = [got[f * PLANE : (f + 1) * PLANE] for f in range(10)]
        lam, shear, inverse = (plane(m_ref, slot, a) for slot in range(3))
        for f, value in enumerate(flux(own, other, lam, shear, inverse, 0, sign)):
            e_ref[pl.ds(f * NODES + a * PLANE, PLANE), :] = plane(e_ref, f, a) + value


def fetch(far, targets):
    high = far.astype(BF16)
    low = (far - high.astype(F32)).astype(BF16)
    picks = (
        lax.broadcasted_iota(jnp.int32, (CELLS, CELLS), 0) == jnp.broadcast_to(targets, (CELLS, CELLS))
    ).astype(F32).astype(BF16)
    return jnp.dot(
        jnp.concatenate([high, low], axis=1),
        jnp.concatenate([picks, picks], axis=0),
        preferred_element_type=F32,
    )


def flux(own, far, lam, shear, inverse, direction, sign):
    jump = [far[f] - own[f] for f in range(9)]
    top = jnp.maximum(own[9], far[9]) * (0.5 * LIFT)
    scale = 0.5 * LIFT * sign
    lam, shear, inverse = lam * scale, shear * scale, inverse * scale
    normal = {0: 6, 1: 7, 2: 8}[direction]
    stress = {0: (0, 3, 5), 1: (3, 1, 4), 2: (5, 4, 2)}[direction]
    out = [top * jump[f] for f in range(9)]
    across = lam * jump[normal]
    for f in range(3):
        out[f] = out[f] + across
    out[direction] = out[direction] + 2.0 * shear * jump[normal]
    for other in range(3):
        if other != direction:
            slot = {(0, 1): 3, (1, 2): 4, (0, 2): 5}[(min(direction, other), max(direction, other))]
            out[slot] = out[slot] + shear * jump[6 + other]
    for other in range(3):
        out[6 + other] = out[6 + other] + inverse * jump[stress[other]]
    return out


def volume_and_faces(i_ref, q0_ref, m_ref, n_ref, k_ref, e_ref, t_ref, x_ref, far_ref):
    slopes(i_ref, k_ref, t_ref, x_ref)
    for a in range(8):
        for field, value in enumerate(elastic_plane(a, t_ref, x_ref, m_ref)):
            at = pl.ds(field * NODES + a * PLANE, PLANE)
            e_ref[at, :] = q0_ref[at, :] + value

    def y_face(ref, slot, place):
        return [ref[pl.ds(slot * NODES + a * PLANE + place * 8, 8), :] for a in range(8)]

    def z_face(ref, slot, place):
        return ref[pl.ds(slot * NODES + place, PLANE, stride=8), :]

    for face in (2, 3):
        own_place, far_place, sign = (0, 7, 1.0) if face % 2 else (7, 0, -1.0)
        targets = n_ref[pl.ds(face, 1), :] & (CELLS - 1)
        far = jnp.concatenate(
            [x for f in range(9) for x in y_face(i_ref, f, far_place)] + y_face(m_ref, 3, far_place), axis=0
        )
        far_ref[...] = fetch(far, targets)
        for a in range(8):
            at = a * PLANE + own_place * 8

            def pick(ref, slot):
                return ref[pl.ds(slot * NODES + at, 8), :]

            own = [pick(i_ref, f) for f in range(9)] + [pick(m_ref, 3)]
            other = [far_ref[pl.ds(f * PLANE + a * 8, 8), :] for f in range(10)]
            for f, value in enumerate(
                flux(own, other, pick(m_ref, 0), pick(m_ref, 1), pick(m_ref, 2), 1, sign)
            ):
                e_ref[pl.ds(f * NODES + at, 8), :] = pick(e_ref, f) + value
    for face in (4, 5):
        own_place, far_place, sign = (0, 7, 1.0) if face % 2 else (7, 0, -1.0)
        targets = n_ref[pl.ds(face, 1), :] & (CELLS - 1)
        far = jnp.concatenate(
            [z_face(i_ref, f, far_place) for f in range(9)] + [z_face(m_ref, 3, far_place)], axis=0
        )
        got = fetch(far, targets)
        own = [z_face(i_ref, f, own_place) for f in range(9)] + [z_face(m_ref, 3, own_place)]
        other = [got[f * PLANE : (f + 1) * PLANE] for f in range(10)]
        for f, value in enumerate(
            flux(own, other, z_face(m_ref, 0, own_place), z_face(m_ref, 1, own_place), z_face(m_ref, 2, own_place), 2, sign)
        ):
            e_ref[pl.ds(f * NODES + own_place, PLANE, stride=8), :] = z_face(e_ref, f, own_place) + value


def finish_kernel(e_ref, out_hbm, out_ref, sem):
    copies = []
    for field in range(9):
        for tile in range(4):
            block = e_ref[pl.ds(field * NODES + tile * 128, 128), :]
            out_ref[field, :, tile * 128 : (tile + 1) * 128] = block.T
        copies.append(pltpu.make_async_copy(out_ref.at[field], out_hbm.at[field], sem.at[field]))
        copies[-1].start()
    for copy in copies:
        copy.wait()


def shape(*dims):
    return jax.ShapeDtypeStruct(dims, F32)


def in_hbm(value):
    return pltpu.with_memory_space_constraint(value, pltpu.MemorySpace.HBM)


def step(solution, material, neighbours, refine_count):
    table = jnp.asarray(plane_table())
    smem = pl.BlockSpec(memory_space=pltpu.SMEM)
    hbm = pl.BlockSpec(memory_space=pltpu.MemorySpace.HBM)

    def field_buffer(count):
        return pltpu.VMEM((count * NODES, CELLS), F32)

    return pl.pallas_call(
        step_kernel,
        out_shape=pltpu.VMEM((9 * NODES, CELLS), F32),
        in_specs=[hbm, hbm, hbm, smem, hbm],
        out_specs=pl.BlockSpec(memory_space=pltpu.VMEM),
        scratch_shapes=[
            pltpu.VMEM((9, CELLS, NODES), F32),
            pltpu.VMEM((3, CELLS, NODES), F32),
            pltpu.VMEM((6, CELLS), jnp.int32),
            pltpu.VMEM((128, 256), F32),
            field_buffer(9),
            field_buffer(9),
            field_buffer(9),
            field_buffer(9),
            field_buffer(4),
            field_buffer(8),
            field_buffer(6),
            pltpu.VMEM((10 * PLANE, CELLS), F32),
            pltpu.VMEM((10 * PLANE, CELLS), F32),
            pltpu.VMEM((10 * PLANE, CELLS), F32),
            pltpu.VMEM((10 * PLANE, CELLS), F32),
            pltpu.VMEM((10 * PLANE, CELLS), F32),
            pltpu.SemaphoreType.DMA((12,)),
            pltpu.SemaphoreType.DMA((2,)),
            pltpu.SemaphoreType.DMA((2,)),
        ],
        compiler_params=pltpu.CompilerParams(
            vmem_limit_bytes=VMEM_LIMIT, collective_id=0, has_side_effects=True
        ),
        name="step",
    )(in_hbm(solution), in_hbm(material), in_hbm(neighbours), refine_count, in_hbm(table))


def finish(nodal):
    return pl.pallas_call(
        finish_kernel,
        out_shape=shape(9, CELLS, NODES),
        in_specs=[pl.BlockSpec(memory_space=pltpu.VMEM)],
        out_specs=pl.BlockSpec(memory_space=pltpu.MemorySpace.HBM),
        scratch_shapes=[pltpu.VMEM((9, CELLS, NODES), F32), pltpu.SemaphoreType.DMA((9,))],
        compiler_params=pltpu.CompilerParams(vmem_limit_bytes=VMEM_LIMIT),
        name="finish",
    )(nodal)


def on_device(solution, material, neighbours, refine_count):
    return finish(step(solution, material, neighbours, refine_count))


def solution(mesh):
    in_specs = (
        P(None, ("space", "help"), None),
        P(None, ("space", "help"), None),
        P(None, ("space", "help")),
        P("space", "help"),
    )
    out_specs = P(None, ("space", "help"), None)
    return jax.shard_map(
        on_device, mesh=mesh, in_specs=in_specs, out_specs=out_specs, check_vma=False
    )
```

```python
import math

import jax
import jax.numpy as jnp
import ml_dtypes
import numpy as np
from jax import lax
from jax.experimental import pallas as pl
from jax.experimental.pallas import tpu as pltpu
from jax.sharding import PartitionSpec as P

ORD = 8
NODES = 512
PLANE = 64
CELLS = 128
STEP = 0.5
LIFT = 0.5
F32 = jnp.float32
BF16 = jnp.bfloat16
VMEM_LIMIT = 32 * 2**20

COLS = (6, 7, 8, 4, 3, 1, 5, 2)
X_FIELDS = (6, 7, 8, 0, 3, 5)


def cheb_table(node_count):
    intervals = node_count - 1
    places = np.arange(node_count)
    points = np.cos(np.pi * places / intervals)
    weights = np.where((places == 0) | (places == intervals), 2.0, 1.0)
    scaled = weights * (-1.0) ** places
    differ = points[:, None] - points[None, :] + np.eye(node_count)
    matrix = np.outer(scaled, 1.0 / scaled) / differ
    matrix = matrix - np.eye(node_count) * np.sum(matrix, axis=1)[:, None]
    return matrix / (node_count * node_count / 4.0)


TABLE = cheb_table(8)
EVEN = [[float((TABLE[i, j] + TABLE[i, 7 - j]) / 2) for j in range(4)] for i in range(4)]
ODD = [[float((TABLE[i, j] - TABLE[i, 7 - j]) / 2) for j in range(4)] for i in range(4)]


def plane_table():
    both = np.concatenate([np.kron(TABLE, np.eye(8)), np.kron(np.eye(8), TABLE)])
    both = both.astype(np.float32)
    high = both.astype(ml_dtypes.bfloat16).astype(np.float32)
    low = (both - high).astype(ml_dtypes.bfloat16).astype(np.float32)
    return np.concatenate([high, high, low, np.zeros_like(low)], axis=1)


def weight(degree):
    return STEP ** (degree + 1) / math.factorial(degree + 1)


def line_derivative(lines):
    plus = [lines[j] + lines[7 - j] for j in range(4)]
    minus = [lines[j] - lines[7 - j] for j in range(4)]
    out = [None] * 8
    for i in range(4):
        first = EVEN[i][0] * plus[0]
        second = ODD[i][0] * minus[0]
        for j in range(1, 4):
            first = first + EVEN[i][j] * plus[j]
            second = second + ODD[i][j] * minus[j]
        out[i] = second + first
        out[7 - i] = second - first
    return out


def plane(ref, slot, a):
    return ref[pl.ds(slot * NODES + a * PLANE, PLANE), :]


def halves(value):
    high = value.astype(BF16)
    low = (value - high.astype(F32)).astype(BF16)
    return high, low


def slopes(q_ref, k_ref, t_ref, x_ref):
    k = k_ref[...].astype(BF16)[:, :192]

    for i in range(8):
        split = {}
        for field in COLS:
            high, low = halves(plane(q_ref, field, i))
            split[field] = jnp.concatenate([high, low, high], axis=0)

        def dot(left, fields):
            right = jnp.concatenate([split[f] for f in fields], axis=1)
            return jnp.dot(left, right, preferred_element_type=F32)

        both = dot(k, (6, 7, 8, 4))
        along_y = dot(k[:64], (3, 1))
        along_z = dot(k[64:], (5, 2))
        for slot, field in enumerate(X_FIELDS):
            lines = [q_ref[pl.ds(field * NODES + a * PLANE + i * 8, 8), :] for a in range(8)]
            for a, value in enumerate(line_derivative(lines)):
                x_ref[pl.ds(slot * NODES + a * PLANE + i * 8, 8), :] = value

        def put(slot, value):
            t_ref[pl.ds(slot * NODES + i * PLANE, PLANE), :] = value

        put(0, both[:64, 128:256])
        put(1, both[64:, 256:384])
        put(2, both[:64, :128])
        put(3, both[64:, 128:256] + both[:64, 256:384])
        put(4, both[64:, :128])
        put(5, along_y[:, :128] + along_z[:, :128])
        put(6, along_y[:, 128:] + both[64:, 384:])
        put(7, both[:64, 384:] + along_z[:, 128:])


def elastic_plane(a, t_ref, x_ref, m_ref, scale=None):
    def t(slot):
        return plane(t_ref, slot, a)

    def x(slot):
        return plane(x_ref, slot, a)

    lam, shear, inverse = (plane(m_ref, slot, a) for slot in range(3))
    if scale is not None:
        lam, shear, inverse = lam * scale, shear * scale, inverse * scale
    twice = shear + shear
    xx, yy, zz = x(0), t(0), t(1)
    spread = lam * (xx + yy + zz)
    return [
        spread + twice * xx,
        spread + twice * yy,
        spread + twice * zz,
        shear * (t(2) + x(1)),
        shear * t(3),
        shear * (t(4) + x(2)),
        inverse * (x(3) + t(5)),
        inverse * (x(4) + t(6)),
        inverse * (x(5) + t(7)),
    ]


def remote(src, dst, send, recv, peer):
    return pltpu.make_async_remote_copy(
        src_ref=src,
        dst_ref=dst,
        send_sem=send,
        recv_sem=recv,
        device_id={"space": peer},
        device_id_type=pl.DeviceIdType.MESH,
    )


def step_kernel(
    sol_hbm, mat_hbm, n_hbm, count_ref, k_hbm,
    e_ref,
    sol_ref, mat_ref, n_ref, k_ref, q0_ref, q_ref, u_ref, i_ref, m_ref, t_ref, x_ref, far_ref,
    sent_ref, got_ref,
    sem, send_sem, recv_sem,
):
    me = lax.axis_index("space")
    peers = lax.axis_size("space")
    right, left = lax.rem(me + 1, peers), lax.rem(me + peers - 1, peers)
    barrier = pltpu.get_barrier_semaphore()
    for peer in (left, right):
        pl.semaphore_signal(barrier, inc=1, device_id={"space": peer}, device_id_type=pl.DeviceIdType.MESH)

    copies = [pltpu.make_async_copy(sol_hbm.at[f], sol_ref.at[f], sem.at[f]) for f in range(9)]
    copies.append(pltpu.make_async_copy(mat_hbm, mat_ref, sem.at[9]))
    copies.append(pltpu.make_async_copy(k_hbm, k_ref, sem.at[10]))
    copies.append(pltpu.make_async_copy(n_hbm, n_ref, sem.at[11]))
    for copy in copies:
        copy.start()
    for field in range(9):
        copies[field].wait()
        for tile in range(4):
            q0_ref[pl.ds(field * NODES + tile * 128, 128), :] = sol_ref[field, :, tile * 128 : (tile + 1) * 128].T
    for copy in copies[9:]:
        copy.wait()
    for tile in range(4):
        span = slice(tile * 128, (tile + 1) * 128)
        density = mat_ref[0, :, span].T
        lam = mat_ref[1, :, span].T
        shear = mat_ref[2, :, span].T
        inverse = 1.0 / density
        for slot, value in enumerate(
            (lam, shear, inverse, jnp.sqrt((lam + 2.0 * shear) / density))
        ):
            m_ref[pl.ds(slot * NODES + tile * 128, 128), :] = value

    slopes(q0_ref, k_ref, t_ref, x_ref)
    for a in range(8):
        for field, value in enumerate(elastic_plane(a, t_ref, x_ref, m_ref)):
            at = pl.ds(field * NODES + a * PLANE, PLANE)
            i_ref[at, :] = weight(0) * plane(q0_ref, field, a) + weight(1) * value
            q_ref[at, :] = value
            u_ref[at, :] = value

    pl.semaphore_wait(barrier, 2)
    sends = [
        remote(sent_ref.at[slot], got_ref.at[slot], send_sem.at[slot], recv_sem.at[slot], (right, left)[slot % 2])
        for slot in range(4)
    ]
    for side, a in enumerate((0, 7)):
        sent_ref[side] = compact(faces(i_ref, m_ref, a), False)
        sends[side].start()

    def nested(turn, scale):
        slopes(u_ref, k_ref, t_ref, x_ref)
        for a in range(8):
            for field, value in enumerate(elastic_plane(a, t_ref, x_ref, m_ref, scale)):
                u_ref[pl.ds(field * NODES + a * PLANE, PLANE), :] = plane(q_ref, field, a) + value
        degree = (7 - turn).astype(F32)
        return scale * ((degree + 1.0) / degree)

    lax.fori_loop(0, ORD - 3, nested, jnp.float32(STEP / ORD))
    slopes(u_ref, k_ref, t_ref, x_ref)
    refined = lax.broadcasted_iota(jnp.int32, (PLANE, CELLS), 1) < count_ref[0, 0]
    for a in range(8):
        for field, value in enumerate(elastic_plane(a, t_ref, x_ref, m_ref, weight(2))):
            at = pl.ds(field * NODES + a * PLANE, PLANE)
            i_ref[at, :] = i_ref[at, :] + jnp.where(refined, value, 0.0)

    for side, a in enumerate((0, 7)):
        sent_ref[2 + side] = compact(faces(i_ref, m_ref, a), True)

    @pl.when(lax.rem(me, 2) == 0)
    def _():
        sends[3].start()
        sends[2].start()

    @pl.when(lax.rem(me, 2) == 1)
    def _():
        sends[2].start()
        sends[3].start()

    volume_and_faces(i_ref, q0_ref, m_ref, n_ref, k_ref, e_ref, t_ref, x_ref, far_ref)

    for send in sends:
        send.wait()
    for face, a, sign in ((0, 7, -1.0), (1, 0, 1.0)):
        got = fetch_compact(got_ref[face], got_ref[2 + face], n_ref[pl.ds(face, 1), :] & (CELLS - 1))
        own = faces(i_ref, m_ref, a)
        other = [got[f * PLANE : (f + 1) * PLANE] for f in range(10)]
        lam, shear, inverse = (plane(m_ref, slot, a) for slot in range(3))
        for f, value in enumerate(flux(own, other, lam, shear, inverse, 0, sign)):
            e_ref[pl.ds(f * NODES + a * PLANE, PLANE), :] = plane(e_ref, f, a) + value


def faces(i_ref, m_ref, a):
    return [plane(i_ref, f, a) for f in range(9)] + [plane(m_ref, 3, a)]


def as_bf16(mask):
    return mask.astype(F32).astype(BF16)


def compact(parts, first):
    row = lax.broadcasted_iota(jnp.int32, (CELLS, CELLS), 0)
    column = lax.broadcasted_iota(jnp.int32, (CELLS, CELLS), 1)
    if first:
        top, bottom = row == jnp.where(column < 64, column, -1), row == column - 64
    else:
        top, bottom = row == column + 64, row == jnp.where(column < 64, -1, column)
    top, bottom = as_bf16(top), as_bf16(bottom)
    values = halves(jnp.concatenate(parts[:5], axis=0)) + halves(jnp.concatenate(parts[5:], axis=0))
    return jnp.dot(
        jnp.concatenate(values, axis=1),
        jnp.concatenate([top, top, bottom, bottom], axis=0),
        preferred_element_type=F32,
    )


def fetch_compact(upper, lower, targets):
    row = lax.broadcasted_iota(jnp.int32, (CELLS, CELLS), 0)
    targets = jnp.broadcast_to(targets, (CELLS, CELLS))
    in_upper = targets >= 64
    picks = [
        jnp.concatenate([as_bf16(row == targets - 64), as_bf16(row == jnp.where(in_upper, targets, -1))], axis=1),
        jnp.concatenate([as_bf16(row == jnp.where(in_upper, -1, targets)), as_bf16(row == targets + 64)], axis=1),
    ]
    values = halves(upper) + halves(lower)
    both = jnp.dot(
        jnp.concatenate(values, axis=1),
        jnp.concatenate([picks[0], picks[0], picks[1], picks[1]], axis=0),
        preferred_element_type=F32,
    )
    return jnp.concatenate([both[:, :CELLS], both[:, CELLS:]], axis=0)


def fetch(far, targets):
    high = far.astype(BF16)
    low = (far - high.astype(F32)).astype(BF16)
    picks = (
        lax.broadcasted_iota(jnp.int32, (CELLS, CELLS), 0) == jnp.broadcast_to(targets, (CELLS, CELLS))
    ).astype(F32).astype(BF16)
    return jnp.dot(
        jnp.concatenate([high, low], axis=1),
        jnp.concatenate([picks, picks], axis=0),
        preferred_element_type=F32,
    )


def flux(own, far, lam, shear, inverse, direction, sign):
    jump = [far[f] - own[f] for f in range(9)]
    top = jnp.maximum(own[9], far[9]) * (0.5 * LIFT)
    scale = 0.5 * LIFT * sign
    lam, shear, inverse = lam * scale, shear * scale, inverse * scale
    normal = {0: 6, 1: 7, 2: 8}[direction]
    stress = {0: (0, 3, 5), 1: (3, 1, 4), 2: (5, 4, 2)}[direction]
    out = [top * jump[f] for f in range(9)]
    across = lam * jump[normal]
    for f in range(3):
        out[f] = out[f] + across
    out[direction] = out[direction] + 2.0 * shear * jump[normal]
    for other in range(3):
        if other != direction:
            slot = {(0, 1): 3, (1, 2): 4, (0, 2): 5}[(min(direction, other), max(direction, other))]
            out[slot] = out[slot] + shear * jump[6 + other]
    for other in range(3):
        out[6 + other] = out[6 + other] + inverse * jump[stress[other]]
    return out


def volume_and_faces(i_ref, q0_ref, m_ref, n_ref, k_ref, e_ref, t_ref, x_ref, far_ref):
    slopes(i_ref, k_ref, t_ref, x_ref)
    for a in range(8):
        for field, value in enumerate(elastic_plane(a, t_ref, x_ref, m_ref)):
            at = pl.ds(field * NODES + a * PLANE, PLANE)
            e_ref[at, :] = q0_ref[at, :] + value

    def y_face(ref, slot, place):
        return [ref[pl.ds(slot * NODES + a * PLANE + place * 8, 8), :] for a in range(8)]

    def z_face(ref, slot, place):
        return ref[pl.ds(slot * NODES + place, PLANE, stride=8), :]

    for face in (2, 3):
        own_place, far_place, sign = (0, 7, 1.0) if face % 2 else (7, 0, -1.0)
        targets = n_ref[pl.ds(face, 1), :] & (CELLS - 1)
        far = jnp.concatenate(
            [x for f in range(9) for x in y_face(i_ref, f, far_place)] + y_face(m_ref, 3, far_place), axis=0
        )
        far_ref[...] = fetch(far, targets)
        for a in range(8):
            at = a * PLANE + own_place * 8

            def pick(ref, slot):
                return ref[pl.ds(slot * NODES + at, 8), :]

            own = [pick(i_ref, f) for f in range(9)] + [pick(m_ref, 3)]
            other = [far_ref[pl.ds(f * PLANE + a * 8, 8), :] for f in range(10)]
            for f, value in enumerate(
                flux(own, other, pick(m_ref, 0), pick(m_ref, 1), pick(m_ref, 2), 1, sign)
            ):
                e_ref[pl.ds(f * NODES + at, 8), :] = pick(e_ref, f) + value
    for face in (4, 5):
        own_place, far_place, sign = (0, 7, 1.0) if face % 2 else (7, 0, -1.0)
        targets = n_ref[pl.ds(face, 1), :] & (CELLS - 1)
        far = jnp.concatenate(
            [z_face(i_ref, f, far_place) for f in range(9)] + [z_face(m_ref, 3, far_place)], axis=0
        )
        got = fetch(far, targets)
        own = [z_face(i_ref, f, own_place) for f in range(9)] + [z_face(m_ref, 3, own_place)]
        other = [got[f * PLANE : (f + 1) * PLANE] for f in range(10)]
        for f, value in enumerate(
            flux(own, other, z_face(m_ref, 0, own_place), z_face(m_ref, 1, own_place), z_face(m_ref, 2, own_place), 2, sign)
        ):
            e_ref[pl.ds(f * NODES + own_place, PLANE, stride=8), :] = z_face(e_ref, f, own_place) + value


def finish_kernel(e_ref, out_hbm, out_ref, sem):
    copies = []
    for field in range(9):
        for tile in range(4):
            block = e_ref[pl.ds(field * NODES + tile * 128, 128), :]
            out_ref[field, :, tile * 128 : (tile + 1) * 128] = block.T
        copies.append(pltpu.make_async_copy(out_ref.at[field], out_hbm.at[field], sem.at[field]))
        copies[-1].start()
    for copy in copies:
        copy.wait()


def shape(*dims):
    return jax.ShapeDtypeStruct(dims, F32)


def in_hbm(value):
    return pltpu.with_memory_space_constraint(value, pltpu.MemorySpace.HBM)


def step(solution, material, neighbours, refine_count):
    table = jnp.asarray(plane_table())
    smem = pl.BlockSpec(memory_space=pltpu.SMEM)
    hbm = pl.BlockSpec(memory_space=pltpu.MemorySpace.HBM)

    def field_buffer(count):
        return pltpu.VMEM((count * NODES, CELLS), F32)

    return pl.pallas_call(
        step_kernel,
        out_shape=pltpu.VMEM((9 * NODES, CELLS), F32),
        in_specs=[hbm, hbm, hbm, smem, hbm],
        out_specs=pl.BlockSpec(memory_space=pltpu.VMEM),
        scratch_shapes=[
            pltpu.VMEM((9, CELLS, NODES), F32),
            pltpu.VMEM((3, CELLS, NODES), F32),
            pltpu.VMEM((6, CELLS), jnp.int32),
            pltpu.VMEM((128, 256), F32),
            field_buffer(9),
            field_buffer(9),
            field_buffer(9),
            field_buffer(9),
            field_buffer(4),
            field_buffer(8),
            field_buffer(6),
            pltpu.VMEM((10 * PLANE, CELLS), F32),
            pltpu.VMEM((4, 5 * PLANE, CELLS), F32),
            pltpu.VMEM((4, 5 * PLANE, CELLS), F32),
            pltpu.SemaphoreType.DMA((12,)),
            pltpu.SemaphoreType.DMA((4,)),
            pltpu.SemaphoreType.DMA((4,)),
        ],
        compiler_params=pltpu.CompilerParams(
            vmem_limit_bytes=VMEM_LIMIT, collective_id=0, has_side_effects=True
        ),
        name="step",
    )(in_hbm(solution), in_hbm(material), in_hbm(neighbours), refine_count, in_hbm(table))


def finish(nodal):
    return pl.pallas_call(
        finish_kernel,
        out_shape=shape(9, CELLS, NODES),
        in_specs=[pl.BlockSpec(memory_space=pltpu.VMEM)],
        out_specs=pl.BlockSpec(memory_space=pltpu.MemorySpace.HBM),
        scratch_shapes=[pltpu.VMEM((9, CELLS, NODES), F32), pltpu.SemaphoreType.DMA((9,))],
        compiler_params=pltpu.CompilerParams(vmem_limit_bytes=VMEM_LIMIT),
        name="finish",
    )(nodal)


def on_device(solution, material, neighbours, refine_count):
    return finish(step(solution, material, neighbours, refine_count))


def solution(mesh):
    in_specs = (
        P(None, ("space", "help"), None),
        P(None, ("space", "help"), None),
        P(None, ("space", "help")),
        P("space", "help"),
    )
    out_specs = P(None, ("space", "help"), None)
    return jax.shard_map(
        on_device, mesh=mesh, in_specs=in_specs, out_specs=out_specs, check_vma=False
    )
```

```python
import math

import jax
import jax.numpy as jnp
import ml_dtypes
import numpy as np
from jax import lax
from jax.experimental import pallas as pl
from jax.experimental.pallas import tpu as pltpu
from jax.sharding import PartitionSpec as P

ORD = 8
NODES = 512
PLANE = 64
CELLS = 128
STEP = 0.5
LIFT = 0.5
F32 = jnp.float32
BF16 = jnp.bfloat16
VMEM_LIMIT = 32 * 2**20

COLS = (6, 7, 8, 4, 3, 1, 5, 2)
X_FIELDS = (6, 7, 8, 0, 3, 5)


def cheb_table(node_count):
    intervals = node_count - 1
    places = np.arange(node_count)
    points = np.cos(np.pi * places / intervals)
    weights = np.where((places == 0) | (places == intervals), 2.0, 1.0)
    scaled = weights * (-1.0) ** places
    differ = points[:, None] - points[None, :] + np.eye(node_count)
    matrix = np.outer(scaled, 1.0 / scaled) / differ
    matrix = matrix - np.eye(node_count) * np.sum(matrix, axis=1)[:, None]
    return matrix / (node_count * node_count / 4.0)


TABLE = cheb_table(8)


def plane_table():
    both = np.concatenate([np.kron(TABLE, np.eye(8)), np.kron(np.eye(8), TABLE)])
    both = both.astype(np.float32)
    high = both.astype(ml_dtypes.bfloat16).astype(np.float32)
    low = (both - high).astype(ml_dtypes.bfloat16).astype(np.float32)
    return np.concatenate([high, high, low, np.zeros_like(low)], axis=1)


def weight(degree):
    return STEP ** (degree + 1) / math.factorial(degree + 1)


def plane(ref, slot, a):
    return ref[pl.ds(slot * NODES + a * PLANE, PLANE), :]


def halves(value):
    high = value.astype(BF16)
    low = (value - high.astype(F32)).astype(BF16)
    return high, low


def matmul_table(k_ref):
    return k_ref[...].astype(BF16)[:, :192]


def triple(value):
    high, low = halves(value)
    return jnp.concatenate([high, low, high], axis=0)


def dot(left, parts):
    return jnp.dot(left, jnp.concatenate(parts, axis=1), preferred_element_type=F32)


def line_slopes(i, k, q_ref, x_ref):
    for first in range(0, 6, 2):
        parts = []
        for field in X_FIELDS[first : first + 2]:
            lines = [q_ref[pl.ds(field * NODES + a * PLANE + i * 8, 8), :] for a in range(8)]
            parts.append(triple(jnp.concatenate(lines, axis=0)))
        along_x = dot(k[:64], parts)
        for place in range(2):
            for a in range(8):
                x_ref[pl.ds((first + place) * NODES + a * PLANE + i * 8, 8), :] = along_x[
                    a * 8 : a * 8 + 8, place * CELLS : (place + 1) * CELLS
                ]


def plane_slopes(i, k, q_ref, t_ref):
    split = {field: triple(plane(q_ref, field, i)) for field in COLS}
    both = dot(k, [split[f] for f in (6, 7, 8, 4)])
    along_y = dot(k[:64], [split[f] for f in (3, 1)])
    along_z = dot(k[64:], [split[f] for f in (5, 2)])

    def put(slot, value):
        t_ref[pl.ds(slot * NODES + i * PLANE, PLANE), :] = value

    put(0, both[:64, 128:256])
    put(1, both[64:, 256:384])
    put(2, both[:64, :128])
    put(3, both[64:, 128:256] + both[:64, 256:384])
    put(4, both[64:, :128])
    put(5, along_y[:, :128] + along_z[:, :128])
    put(6, along_y[:, 128:] + both[64:, 384:])
    put(7, both[:64, 384:] + along_z[:, 128:])


def slopes(q_ref, k_ref, t_ref, x_ref):
    k = matmul_table(k_ref)
    for i in range(8):
        plane_slopes(i, k, q_ref, t_ref)
        line_slopes(i, k, q_ref, x_ref)


def elastic_plane(a, t_ref, x_ref, m_ref, scale=None):
    def t(slot):
        return plane(t_ref, slot, a)

    def x(slot):
        return plane(x_ref, slot, a)

    lam, shear, inverse = (plane(m_ref, slot, a) for slot in range(3))
    if scale is not None:
        lam, shear, inverse = lam * scale, shear * scale, inverse * scale
    twice = shear + shear
    xx, yy, zz = x(0), t(0), t(1)
    spread = lam * (xx + yy + zz)
    return [
        spread + twice * xx,
        spread + twice * yy,
        spread + twice * zz,
        shear * (t(2) + x(1)),
        shear * t(3),
        shear * (t(4) + x(2)),
        inverse * (x(3) + t(5)),
        inverse * (x(4) + t(6)),
        inverse * (x(5) + t(7)),
    ]


def remote(src, dst, send, recv, peer):
    return pltpu.make_async_remote_copy(
        src_ref=src,
        dst_ref=dst,
        send_sem=send,
        recv_sem=recv,
        device_id={"space": peer},
        device_id_type=pl.DeviceIdType.MESH,
    )


def step_kernel(
    sol_hbm, mat_hbm, n_hbm, count_ref, k_hbm,
    e_ref, middle_ref,
    sol_ref, mat_ref, n_ref, k_ref, q0_ref, q_ref, u_ref, i_ref, m_ref, t_ref, x_ref, far_ref,
    sent_ref, got_ref,
    sem, send_sem, recv_sem,
):
    me = lax.axis_index("space")
    peers = lax.axis_size("space")
    right, left = lax.rem(me + 1, peers), lax.rem(me + peers - 1, peers)
    barrier = pltpu.get_barrier_semaphore()
    for peer in (left, right):
        pl.semaphore_signal(barrier, inc=1, device_id={"space": peer}, device_id_type=pl.DeviceIdType.MESH)

    copies = [pltpu.make_async_copy(sol_hbm.at[f], sol_ref.at[f], sem.at[f]) for f in range(9)]
    copies.append(pltpu.make_async_copy(mat_hbm, mat_ref, sem.at[9]))
    copies.append(pltpu.make_async_copy(k_hbm, k_ref, sem.at[10]))
    copies.append(pltpu.make_async_copy(n_hbm, n_ref, sem.at[11]))
    for copy in copies:
        copy.start()
    for field in range(9):
        copies[field].wait()
        for tile in range(4):
            q0_ref[pl.ds(field * NODES + tile * 128, 128), :] = sol_ref[field, :, tile * 128 : (tile + 1) * 128].T
    for copy in copies[9:]:
        copy.wait()
    for tile in range(4):
        span = slice(tile * 128, (tile + 1) * 128)
        density = mat_ref[0, :, span].T
        lam = mat_ref[1, :, span].T
        shear = mat_ref[2, :, span].T
        inverse = 1.0 / density
        for slot, value in enumerate(
            (lam, shear, inverse, jnp.sqrt((lam + 2.0 * shear) / density))
        ):
            m_ref[pl.ds(slot * NODES + tile * 128, 128), :] = value

    slopes(q0_ref, k_ref, t_ref, x_ref)
    for a in range(8):
        for field, value in enumerate(elastic_plane(a, t_ref, x_ref, m_ref)):
            at = pl.ds(field * NODES + a * PLANE, PLANE)
            i_ref[at, :] = weight(0) * plane(q0_ref, field, a) + weight(1) * value
            q_ref[at, :] = value
            u_ref[at, :] = value

    pl.semaphore_wait(barrier, 2)
    sends = [
        remote(sent_ref.at[slot], got_ref.at[slot], send_sem.at[slot], recv_sem.at[slot], (right, left)[slot % 2])
        for slot in range(4)
    ]
    for side, a in enumerate((0, 7)):
        sent_ref[side] = compact(faces(i_ref, m_ref, a), False)
        sends[side].start()

    def nested(turn, scale):
        slopes(u_ref, k_ref, t_ref, x_ref)
        for a in range(8):
            for field, value in enumerate(elastic_plane(a, t_ref, x_ref, m_ref, scale)):
                u_ref[pl.ds(field * NODES + a * PLANE, PLANE), :] = plane(q_ref, field, a) + value
        degree = (7 - turn).astype(F32)
        return scale * ((degree + 1.0) / degree)

    lax.fori_loop(0, ORD - 3, nested, jnp.float32(STEP / ORD))
    refined = lax.broadcasted_iota(jnp.int32, (PLANE, CELLS), 1) < count_ref[0, 0]
    k = matmul_table(k_ref)

    def add_extra(a):
        plane_slopes(a, k, u_ref, t_ref)
        for field, value in enumerate(elastic_plane(a, t_ref, x_ref, m_ref, weight(2))):
            at = pl.ds(field * NODES + a * PLANE, PLANE)
            i_ref[at, :] = i_ref[at, :] + jnp.where(refined, value, 0.0)

    for i in range(8):
        line_slopes(i, k, u_ref, x_ref)
    for a in (0, 7):
        add_extra(a)
    for side, a in enumerate((0, 7)):
        sent_ref[2 + side] = compact(faces(i_ref, m_ref, a), True)

    @pl.when(lax.rem(me, 2) == 0)
    def _():
        sends[3].start()
        sends[2].start()

    @pl.when(lax.rem(me, 2) == 1)
    def _():
        sends[2].start()
        sends[3].start()

    for a in range(1, 7):
        add_extra(a)
    volume_and_faces(i_ref, q0_ref, m_ref, n_ref, k_ref, e_ref, t_ref, x_ref, far_ref)

    for field in range(9):
        for tile in (1, 2):
            middle_ref[field, :, (tile - 1) * 128 : tile * 128] = e_ref[pl.ds(field * NODES + tile * 128, 128), :].T
    for send in sends:
        send.wait()
    for face, a, sign in ((0, 7, -1.0), (1, 0, 1.0)):
        got = fetch_compact(got_ref[face], got_ref[2 + face], n_ref[pl.ds(face, 1), :] & (CELLS - 1))
        own = faces(i_ref, m_ref, a)
        other = [got[f * PLANE : (f + 1) * PLANE] for f in range(10)]
        lam, shear, inverse = (plane(m_ref, slot, a) for slot in range(3))
        for f, value in enumerate(flux(own, other, lam, shear, inverse, 0, sign)):
            e_ref[pl.ds(f * NODES + a * PLANE, PLANE), :] = plane(e_ref, f, a) + value


def faces(i_ref, m_ref, a):
    return [plane(i_ref, f, a) for f in range(9)] + [plane(m_ref, 3, a)]


def as_bf16(mask):
    return mask.astype(F32).astype(BF16)


def compact(parts, first):
    row = lax.broadcasted_iota(jnp.int32, (CELLS, CELLS), 0)
    column = lax.broadcasted_iota(jnp.int32, (CELLS, CELLS), 1)
    if first:
        top, bottom = row == jnp.where(column < 64, column, -1), row == column - 64
    else:
        top, bottom = row == column + 64, row == jnp.where(column < 64, -1, column)
    top, bottom = as_bf16(top), as_bf16(bottom)
    values = halves(jnp.concatenate(parts[:5], axis=0)) + halves(jnp.concatenate(parts[5:], axis=0))
    return jnp.dot(
        jnp.concatenate(values, axis=1),
        jnp.concatenate([top, top, bottom, bottom], axis=0),
        preferred_element_type=F32,
    )


def fetch_compact(upper, lower, targets):
    row = lax.broadcasted_iota(jnp.int32, (CELLS, CELLS), 0)
    targets = jnp.broadcast_to(targets, (CELLS, CELLS))
    in_upper = targets >= 64
    picks = [
        jnp.concatenate([as_bf16(row == targets - 64), as_bf16(row == jnp.where(in_upper, targets, -1))], axis=1),
        jnp.concatenate([as_bf16(row == jnp.where(in_upper, -1, targets)), as_bf16(row == targets + 64)], axis=1),
    ]
    values = halves(upper) + halves(lower)
    both = jnp.dot(
        jnp.concatenate(values, axis=1),
        jnp.concatenate([picks[0], picks[0], picks[1], picks[1]], axis=0),
        preferred_element_type=F32,
    )
    return jnp.concatenate([both[:, :CELLS], both[:, CELLS:]], axis=0)


def fetch(far, targets):
    high = far.astype(BF16)
    low = (far - high.astype(F32)).astype(BF16)
    picks = (
        lax.broadcasted_iota(jnp.int32, (CELLS, CELLS), 0) == jnp.broadcast_to(targets, (CELLS, CELLS))
    ).astype(F32).astype(BF16)
    return jnp.dot(
        jnp.concatenate([high, low], axis=1),
        jnp.concatenate([picks, picks], axis=0),
        preferred_element_type=F32,
    )


def flux(own, far, lam, shear, inverse, direction, sign):
    jump = [far[f] - own[f] for f in range(9)]
    top = jnp.maximum(own[9], far[9]) * (0.5 * LIFT)
    scale = 0.5 * LIFT * sign
    lam, shear, inverse = lam * scale, shear * scale, inverse * scale
    normal = {0: 6, 1: 7, 2: 8}[direction]
    stress = {0: (0, 3, 5), 1: (3, 1, 4), 2: (5, 4, 2)}[direction]
    out = [top * jump[f] for f in range(9)]
    across = lam * jump[normal]
    for f in range(3):
        out[f] = out[f] + across
    out[direction] = out[direction] + 2.0 * shear * jump[normal]
    for other in range(3):
        if other != direction:
            slot = {(0, 1): 3, (1, 2): 4, (0, 2): 5}[(min(direction, other), max(direction, other))]
            out[slot] = out[slot] + shear * jump[6 + other]
    for other in range(3):
        out[6 + other] = out[6 + other] + inverse * jump[stress[other]]
    return out


def volume_and_faces(i_ref, q0_ref, m_ref, n_ref, k_ref, e_ref, t_ref, x_ref, far_ref):
    slopes(i_ref, k_ref, t_ref, x_ref)
    for a in range(8):
        for field, value in enumerate(elastic_plane(a, t_ref, x_ref, m_ref)):
            at = pl.ds(field * NODES + a * PLANE, PLANE)
            e_ref[at, :] = q0_ref[at, :] + value

    def y_face(ref, slot, place):
        return [ref[pl.ds(slot * NODES + a * PLANE + place * 8, 8), :] for a in range(8)]

    def z_face(ref, slot, place):
        return ref[pl.ds(slot * NODES + place, PLANE, stride=8), :]

    for face in (2, 3):
        own_place, far_place, sign = (0, 7, 1.0) if face % 2 else (7, 0, -1.0)
        targets = n_ref[pl.ds(face, 1), :] & (CELLS - 1)
        far = jnp.concatenate(
            [x for f in range(9) for x in y_face(i_ref, f, far_place)] + y_face(m_ref, 3, far_place), axis=0
        )
        far_ref[...] = fetch(far, targets)
        for a in range(8):
            at = a * PLANE + own_place * 8

            def pick(ref, slot):
                return ref[pl.ds(slot * NODES + at, 8), :]

            own = [pick(i_ref, f) for f in range(9)] + [pick(m_ref, 3)]
            other = [far_ref[pl.ds(f * PLANE + a * 8, 8), :] for f in range(10)]
            for f, value in enumerate(
                flux(own, other, pick(m_ref, 0), pick(m_ref, 1), pick(m_ref, 2), 1, sign)
            ):
                e_ref[pl.ds(f * NODES + at, 8), :] = pick(e_ref, f) + value
    for face in (4, 5):
        own_place, far_place, sign = (0, 7, 1.0) if face % 2 else (7, 0, -1.0)
        targets = n_ref[pl.ds(face, 1), :] & (CELLS - 1)
        far = jnp.concatenate(
            [z_face(i_ref, f, far_place) for f in range(9)] + [z_face(m_ref, 3, far_place)], axis=0
        )
        got = fetch(far, targets)
        own = [z_face(i_ref, f, own_place) for f in range(9)] + [z_face(m_ref, 3, own_place)]
        other = [got[f * PLANE : (f + 1) * PLANE] for f in range(10)]
        for f, value in enumerate(
            flux(own, other, z_face(m_ref, 0, own_place), z_face(m_ref, 1, own_place), z_face(m_ref, 2, own_place), 2, sign)
        ):
            e_ref[pl.ds(f * NODES + own_place, PLANE, stride=8), :] = z_face(e_ref, f, own_place) + value


def finish_kernel(e_ref, middle_ref, out_hbm, out_ref, sem):
    def writing(source, columns, field, slot):
        return pltpu.make_async_copy(source, out_hbm.at[field, :, columns], sem.at[slot * 9 + field])

    copies = [writing(middle_ref.at[f], pl.ds(128, 256), f, 0) for f in range(9)]
    for copy in copies:
        copy.start()
    for field in range(9):
        for side, tile in enumerate((0, 3)):
            out_ref[2 * field + side] = e_ref[pl.ds(field * NODES + tile * 128, 128), :].T
            copies.append(writing(out_ref.at[2 * field + side], pl.ds(tile * 128, 128), field, 1 + side))
            copies[-1].start()
    for copy in copies:
        copy.wait()


def shape(*dims):
    return jax.ShapeDtypeStruct(dims, F32)


def in_hbm(value):
    return pltpu.with_memory_space_constraint(value, pltpu.MemorySpace.HBM)


def step(solution, material, neighbours, refine_count):
    table = jnp.asarray(plane_table())
    smem = pl.BlockSpec(memory_space=pltpu.SMEM)
    hbm = pl.BlockSpec(memory_space=pltpu.MemorySpace.HBM)

    def field_buffer(count):
        return pltpu.VMEM((count * NODES, CELLS), F32)

    return pl.pallas_call(
        step_kernel,
        out_shape=(pltpu.VMEM((9 * NODES, CELLS), F32), pltpu.VMEM((9, CELLS, 256), F32)),
        in_specs=[hbm, hbm, hbm, smem, hbm],
        out_specs=[pl.BlockSpec(memory_space=pltpu.VMEM)] * 2,
        scratch_shapes=[
            pltpu.VMEM((9, CELLS, NODES), F32),
            pltpu.VMEM((3, CELLS, NODES), F32),
            pltpu.VMEM((6, CELLS), jnp.int32),
            pltpu.VMEM((128, 256), F32),
            field_buffer(9),
            field_buffer(9),
            field_buffer(9),
            field_buffer(9),
            field_buffer(4),
            field_buffer(8),
            field_buffer(6),
            pltpu.VMEM((10 * PLANE, CELLS), F32),
            pltpu.VMEM((4, 5 * PLANE, CELLS), F32),
            pltpu.VMEM((4, 5 * PLANE, CELLS), F32),
            pltpu.SemaphoreType.DMA((12,)),
            pltpu.SemaphoreType.DMA((4,)),
            pltpu.SemaphoreType.DMA((4,)),
        ],
        compiler_params=pltpu.CompilerParams(
            vmem_limit_bytes=VMEM_LIMIT, collective_id=0, has_side_effects=True
        ),
        name="step",
    )(in_hbm(solution), in_hbm(material), in_hbm(neighbours), refine_count, in_hbm(table))


def finish(nodal, middle):
    return pl.pallas_call(
        finish_kernel,
        out_shape=shape(9, CELLS, NODES),
        in_specs=[pl.BlockSpec(memory_space=pltpu.VMEM)] * 2,
        out_specs=pl.BlockSpec(memory_space=pltpu.MemorySpace.HBM),
        scratch_shapes=[pltpu.VMEM((18, CELLS, 128), F32), pltpu.SemaphoreType.DMA((27,))],
        compiler_params=pltpu.CompilerParams(vmem_limit_bytes=VMEM_LIMIT),
        name="finish",
    )(nodal, middle)


def on_device(solution, material, neighbours, refine_count):
    return finish(*step(solution, material, neighbours, refine_count))


def solution(mesh):
    in_specs = (
        P(None, ("space", "help"), None),
        P(None, ("space", "help"), None),
        P(None, ("space", "help")),
        P("space", "help"),
    )
    out_specs = P(None, ("space", "help"), None)
    return jax.shard_map(
        on_device, mesh=mesh, in_specs=in_specs, out_specs=out_specs, check_vma=False
    )
```

```python
import math

import jax
import jax.numpy as jnp
import ml_dtypes
import numpy as np
from jax import lax
from jax.experimental import pallas as pl
from jax.experimental.pallas import tpu as pltpu
from jax.sharding import PartitionSpec as P

ORD = 8
NODES = 512
PLANE = 64
CELLS = 128
STEP = 0.5
LIFT = 0.5
F32 = jnp.float32
BF16 = jnp.bfloat16
VMEM_LIMIT = 32 * 2**20

COLS = (6, 7, 8, 4, 3, 1, 5, 2)
X_FIELDS = (6, 7, 8, 0, 3, 5)


def cheb_table(node_count):
    intervals = node_count - 1
    places = np.arange(node_count)
    points = np.cos(np.pi * places / intervals)
    weights = np.where((places == 0) | (places == intervals), 2.0, 1.0)
    scaled = weights * (-1.0) ** places
    differ = points[:, None] - points[None, :] + np.eye(node_count)
    matrix = np.outer(scaled, 1.0 / scaled) / differ
    matrix = matrix - np.eye(node_count) * np.sum(matrix, axis=1)[:, None]
    return matrix / (node_count * node_count / 4.0)


TABLE = cheb_table(8)


def plane_table():
    both = np.concatenate([np.kron(TABLE, np.eye(8)), np.kron(np.eye(8), TABLE)])
    both = both.astype(np.float32)
    high = both.astype(ml_dtypes.bfloat16).astype(np.float32)
    low = (both - high).astype(ml_dtypes.bfloat16).astype(np.float32)
    return np.concatenate([high, high, low, np.zeros_like(low)], axis=1)


def weight(degree):
    return STEP ** (degree + 1) / math.factorial(degree + 1)


def plane(ref, slot, a):
    return ref[pl.ds(slot * NODES + a * PLANE, PLANE), :]


def halves(value):
    high = value.astype(BF16)
    low = (value - high.astype(F32)).astype(BF16)
    return high, low


def matmul_table(k_ref):
    return k_ref[...].astype(BF16)[:, :192]


def triple(value):
    high, low = halves(value)
    return jnp.concatenate([high, low, high], axis=0)


def dot(left, parts):
    return jnp.dot(left, jnp.concatenate(parts, axis=1), preferred_element_type=F32)


def line_slopes(i, k, q_ref, x_ref):
    for first in range(0, 6, 2):
        parts = []
        for field in X_FIELDS[first : first + 2]:
            lines = [q_ref[pl.ds(field * NODES + a * PLANE + i * 8, 8), :] for a in range(8)]
            parts.append(triple(jnp.concatenate(lines, axis=0)))
        along_x = dot(k[:64], parts)
        for place in range(2):
            for a in range(8):
                x_ref[pl.ds((first + place) * NODES + a * PLANE + i * 8, 8), :] = along_x[
                    a * 8 : a * 8 + 8, place * CELLS : (place + 1) * CELLS
                ]


def plane_slopes(i, k, q_ref, t_ref):
    def put(slot, value):
        t_ref[pl.ds(slot * NODES + i * PLANE, PLANE), :] = value

    def part(field):
        return triple(plane(q_ref, field, i))

    one = dot(k, [part(6), part(7)])
    put(2, one[:64, :128])
    put(4, one[64:, :128])
    put(0, one[:64, 128:])
    put(3, one[64:, 128:])
    two = dot(k, [part(8), part(4)])
    put(1, two[64:, :128])
    put(3, plane(t_ref, 3, i) + two[:64, :128])
    put(7, two[:64, 128:])
    put(6, two[64:, 128:])
    along_y = dot(k[:64], [part(3), part(1)])
    along_z = dot(k[64:], [part(5), part(2)])
    put(5, along_y[:, :128] + along_z[:, :128])
    put(6, plane(t_ref, 6, i) + along_y[:, 128:])
    put(7, plane(t_ref, 7, i) + along_z[:, 128:])


def slopes(q_ref, k_ref, t_ref, x_ref):
    k = matmul_table(k_ref)
    for i in range(8):
        line_slopes(i, k, q_ref, x_ref)
    for i in range(8):
        plane_slopes(i, k, q_ref, t_ref)


def elastic_plane(a, t_ref, x_ref, m_ref, scale=None):
    def t(slot):
        return plane(t_ref, slot, a)

    def x(slot):
        return plane(x_ref, slot, a)

    lam, shear, inverse = (plane(m_ref, slot, a) for slot in range(3))
    if scale is not None:
        lam, shear, inverse = lam * scale, shear * scale, inverse * scale
    twice = shear + shear
    xx, yy, zz = x(0), t(0), t(1)
    spread = lam * (xx + yy + zz)
    return [
        spread + twice * xx,
        spread + twice * yy,
        spread + twice * zz,
        shear * (t(2) + x(1)),
        shear * t(3),
        shear * (t(4) + x(2)),
        inverse * (x(3) + t(5)),
        inverse * (x(4) + t(6)),
        inverse * (x(5) + t(7)),
    ]


def remote(src, dst, send, recv, peer):
    return pltpu.make_async_remote_copy(
        src_ref=src,
        dst_ref=dst,
        send_sem=send,
        recv_sem=recv,
        device_id={"space": peer},
        device_id_type=pl.DeviceIdType.MESH,
    )


def step_kernel(
    sol_hbm, mat_hbm, n_hbm, count_ref, k_hbm,
    e_ref, middle_ref,
    sol_ref, mat_ref, n_ref, k_ref, q0_ref, q_ref, u_ref, i_ref, m_ref, t_ref, x_ref, far_ref,
    sent_ref, got_ref,
    sem, send_sem, recv_sem,
):
    me = lax.axis_index("space")
    peers = lax.axis_size("space")
    right, left = lax.rem(me + 1, peers), lax.rem(me + peers - 1, peers)
    barrier = pltpu.get_barrier_semaphore()
    for peer in (left, right):
        pl.semaphore_signal(barrier, inc=1, device_id={"space": peer}, device_id_type=pl.DeviceIdType.MESH)

    copies = [pltpu.make_async_copy(sol_hbm.at[f], sol_ref.at[f], sem.at[f]) for f in range(9)]
    copies.append(pltpu.make_async_copy(mat_hbm, mat_ref, sem.at[9]))
    copies.append(pltpu.make_async_copy(k_hbm, k_ref, sem.at[10]))
    copies.append(pltpu.make_async_copy(n_hbm, n_ref, sem.at[11]))
    for copy in copies:
        copy.start()
    for field in range(9):
        copies[field].wait()
        for tile in range(4):
            q0_ref[pl.ds(field * NODES + tile * 128, 128), :] = sol_ref[field, :, tile * 128 : (tile + 1) * 128].T
    for copy in copies[9:]:
        copy.wait()
    for tile in range(4):
        span = slice(tile * 128, (tile + 1) * 128)
        density = mat_ref[0, :, span].T
        lam = mat_ref[1, :, span].T
        shear = mat_ref[2, :, span].T
        inverse = 1.0 / density
        for slot, value in enumerate(
            (lam, shear, inverse, jnp.sqrt((lam + 2.0 * shear) / density))
        ):
            m_ref[pl.ds(slot * NODES + tile * 128, 128), :] = value

    slopes(q0_ref, k_ref, t_ref, x_ref)
    for a in range(8):
        for field, value in enumerate(elastic_plane(a, t_ref, x_ref, m_ref)):
            at = pl.ds(field * NODES + a * PLANE, PLANE)
            i_ref[at, :] = weight(0) * plane(q0_ref, field, a) + weight(1) * value
            q_ref[at, :] = value
            u_ref[at, :] = value

    pl.semaphore_wait(barrier, 2)
    sends = [
        remote(sent_ref.at[slot], got_ref.at[slot], send_sem.at[slot], recv_sem.at[slot], (right, left)[slot % 2])
        for slot in range(4)
    ]
    for side, a in enumerate((0, 7)):
        sent_ref[side] = compact(faces(i_ref, m_ref, a), False)
        sends[side].start()

    def nested(turn, scale):
        slopes(u_ref, k_ref, t_ref, x_ref)
        for a in range(8):
            for field, value in enumerate(elastic_plane(a, t_ref, x_ref, m_ref, scale)):
                u_ref[pl.ds(field * NODES + a * PLANE, PLANE), :] = plane(q_ref, field, a) + value
        degree = (7 - turn).astype(F32)
        return scale * ((degree + 1.0) / degree)

    lax.fori_loop(0, ORD - 3, nested, jnp.float32(STEP / ORD))
    refined = lax.broadcasted_iota(jnp.int32, (PLANE, CELLS), 1) < count_ref[0, 0]
    k = matmul_table(k_ref)

    def add_extra(a):
        plane_slopes(a, k, u_ref, t_ref)
        for field, value in enumerate(elastic_plane(a, t_ref, x_ref, m_ref, weight(2))):
            at = pl.ds(field * NODES + a * PLANE, PLANE)
            i_ref[at, :] = i_ref[at, :] + jnp.where(refined, value, 0.0)

    for i in range(8):
        line_slopes(i, k, u_ref, x_ref)
    for side, a in enumerate((0, 7)):
        add_extra(a)
        sent_ref[2 + side] = compact(faces(i_ref, m_ref, a), True)
        sends[2 + side].start()

    for a in range(1, 7):
        add_extra(a)
    volume_and_faces(i_ref, q0_ref, m_ref, n_ref, k_ref, e_ref, t_ref, x_ref, far_ref)

    for field in range(9):
        for tile in (1, 2):
            middle_ref[field, :, (tile - 1) * 128 : tile * 128] = e_ref[pl.ds(field * NODES + tile * 128, 128), :].T
    for send in sends:
        send.wait()
    for face, a, sign in ((0, 7, -1.0), (1, 0, 1.0)):
        got = fetch_compact(got_ref[face], got_ref[2 + face], n_ref[pl.ds(face, 1), :] & (CELLS - 1))
        own = faces(i_ref, m_ref, a)
        other = [got[f * PLANE : (f + 1) * PLANE] for f in range(10)]
        lam, shear, inverse = (plane(m_ref, slot, a) for slot in range(3))
        for f, value in enumerate(flux(own, other, lam, shear, inverse, 0, sign)):
            e_ref[pl.ds(f * NODES + a * PLANE, PLANE), :] = plane(e_ref, f, a) + value


def faces(i_ref, m_ref, a):
    return [plane(i_ref, f, a) for f in range(9)] + [plane(m_ref, 3, a)]


def as_bf16(mask):
    return mask.astype(F32).astype(BF16)


def compact(parts, first):
    row = lax.broadcasted_iota(jnp.int32, (CELLS, CELLS), 0)
    column = lax.broadcasted_iota(jnp.int32, (CELLS, CELLS), 1)
    if first:
        top, bottom = row == jnp.where(column < 64, column, -1), row == column - 64
    else:
        top, bottom = row == column + 64, row == jnp.where(column < 64, -1, column)
    top, bottom = as_bf16(top), as_bf16(bottom)
    values = halves(jnp.concatenate(parts[:5], axis=0)) + halves(jnp.concatenate(parts[5:], axis=0))
    return jnp.dot(
        jnp.concatenate(values, axis=1),
        jnp.concatenate([top, top, bottom, bottom], axis=0),
        preferred_element_type=F32,
    )


def fetch_compact(upper, lower, targets):
    row = lax.broadcasted_iota(jnp.int32, (CELLS, CELLS), 0)
    targets = jnp.broadcast_to(targets, (CELLS, CELLS))
    in_upper = targets >= 64
    picks = [
        jnp.concatenate([as_bf16(row == targets - 64), as_bf16(row == jnp.where(in_upper, targets, -1))], axis=1),
        jnp.concatenate([as_bf16(row == jnp.where(in_upper, -1, targets)), as_bf16(row == targets + 64)], axis=1),
    ]
    values = halves(upper) + halves(lower)
    both = jnp.dot(
        jnp.concatenate(values, axis=1),
        jnp.concatenate([picks[0], picks[0], picks[1], picks[1]], axis=0),
        preferred_element_type=F32,
    )
    return jnp.concatenate([both[:, :CELLS], both[:, CELLS:]], axis=0)


def fetch(far, targets):
    high = far.astype(BF16)
    low = (far - high.astype(F32)).astype(BF16)
    picks = (
        lax.broadcasted_iota(jnp.int32, (CELLS, CELLS), 0) == jnp.broadcast_to(targets, (CELLS, CELLS))
    ).astype(F32).astype(BF16)
    return jnp.dot(
        jnp.concatenate([high, low], axis=1),
        jnp.concatenate([picks, picks], axis=0),
        preferred_element_type=F32,
    )


def flux(own, far, lam, shear, inverse, direction, sign):
    jump = [far[f] - own[f] for f in range(9)]
    top = jnp.maximum(own[9], far[9]) * (0.5 * LIFT)
    scale = 0.5 * LIFT * sign
    lam, shear, inverse = lam * scale, shear * scale, inverse * scale
    normal = {0: 6, 1: 7, 2: 8}[direction]
    stress = {0: (0, 3, 5), 1: (3, 1, 4), 2: (5, 4, 2)}[direction]
    out = [top * jump[f] for f in range(9)]
    across = lam * jump[normal]
    for f in range(3):
        out[f] = out[f] + across
    out[direction] = out[direction] + 2.0 * shear * jump[normal]
    for other in range(3):
        if other != direction:
            slot = {(0, 1): 3, (1, 2): 4, (0, 2): 5}[(min(direction, other), max(direction, other))]
            out[slot] = out[slot] + shear * jump[6 + other]
    for other in range(3):
        out[6 + other] = out[6 + other] + inverse * jump[stress[other]]
    return out


def volume_and_faces(i_ref, q0_ref, m_ref, n_ref, k_ref, e_ref, t_ref, x_ref, far_ref):
    slopes(i_ref, k_ref, t_ref, x_ref)
    for a in range(8):
        for field, value in enumerate(elastic_plane(a, t_ref, x_ref, m_ref)):
            at = pl.ds(field * NODES + a * PLANE, PLANE)
            e_ref[at, :] = q0_ref[at, :] + value

    def y_face(ref, slot, place):
        return [ref[pl.ds(slot * NODES + a * PLANE + place * 8, 8), :] for a in range(8)]

    def z_face(ref, slot, place):
        return ref[pl.ds(slot * NODES + place, PLANE, stride=8), :]

    for face in (2, 3):
        own_place, far_place, sign = (0, 7, 1.0) if face % 2 else (7, 0, -1.0)
        targets = n_ref[pl.ds(face, 1), :] & (CELLS - 1)
        far = jnp.concatenate(
            [x for f in range(9) for x in y_face(i_ref, f, far_place)] + y_face(m_ref, 3, far_place), axis=0
        )
        far_ref[...] = fetch(far, targets)
        for a in range(8):
            at = a * PLANE + own_place * 8

            def pick(ref, slot):
                return ref[pl.ds(slot * NODES + at, 8), :]

            own = [pick(i_ref, f) for f in range(9)] + [pick(m_ref, 3)]
            other = [far_ref[pl.ds(f * PLANE + a * 8, 8), :] for f in range(10)]
            for f, value in enumerate(
                flux(own, other, pick(m_ref, 0), pick(m_ref, 1), pick(m_ref, 2), 1, sign)
            ):
                e_ref[pl.ds(f * NODES + at, 8), :] = pick(e_ref, f) + value
    for face in (4, 5):
        own_place, far_place, sign = (0, 7, 1.0) if face % 2 else (7, 0, -1.0)
        targets = n_ref[pl.ds(face, 1), :] & (CELLS - 1)
        far = jnp.concatenate(
            [z_face(i_ref, f, far_place) for f in range(9)] + [z_face(m_ref, 3, far_place)], axis=0
        )
        got = fetch(far, targets)
        own = [z_face(i_ref, f, own_place) for f in range(9)] + [z_face(m_ref, 3, own_place)]
        other = [got[f * PLANE : (f + 1) * PLANE] for f in range(10)]
        for f, value in enumerate(
            flux(own, other, z_face(m_ref, 0, own_place), z_face(m_ref, 1, own_place), z_face(m_ref, 2, own_place), 2, sign)
        ):
            e_ref[pl.ds(f * NODES + own_place, PLANE, stride=8), :] = z_face(e_ref, f, own_place) + value


def finish_kernel(e_ref, middle_ref, out_hbm, out_ref, sem):
    def writing(source, columns, field, slot):
        return pltpu.make_async_copy(source, out_hbm.at[field, :, columns], sem.at[slot * 9 + field])

    copies = [writing(middle_ref.at[f], pl.ds(128, 256), f, 0) for f in range(9)]
    for copy in copies:
        copy.start()
    for field in range(9):
        for side, tile in enumerate((0, 3)):
            out_ref[2 * field + side] = e_ref[pl.ds(field * NODES + tile * 128, 128), :].T
            copies.append(writing(out_ref.at[2 * field + side], pl.ds(tile * 128, 128), field, 1 + side))
            copies[-1].start()
    for copy in copies:
        copy.wait()


def shape(*dims):
    return jax.ShapeDtypeStruct(dims, F32)


def in_hbm(value):
    return pltpu.with_memory_space_constraint(value, pltpu.MemorySpace.HBM)


def step(solution, material, neighbours, refine_count):
    table = jnp.asarray(plane_table())
    smem = pl.BlockSpec(memory_space=pltpu.SMEM)
    hbm = pl.BlockSpec(memory_space=pltpu.MemorySpace.HBM)

    def field_buffer(count):
        return pltpu.VMEM((count * NODES, CELLS), F32)

    return pl.pallas_call(
        step_kernel,
        out_shape=(pltpu.VMEM((9 * NODES, CELLS), F32), pltpu.VMEM((9, CELLS, 256), F32)),
        in_specs=[hbm, hbm, hbm, smem, hbm],
        out_specs=[pl.BlockSpec(memory_space=pltpu.VMEM)] * 2,
        scratch_shapes=[
            pltpu.VMEM((9, CELLS, NODES), F32),
            pltpu.VMEM((3, CELLS, NODES), F32),
            pltpu.VMEM((6, CELLS), jnp.int32),
            pltpu.VMEM((128, 256), F32),
            field_buffer(9),
            field_buffer(9),
            field_buffer(9),
            field_buffer(9),
            field_buffer(4),
            field_buffer(8),
            field_buffer(6),
            pltpu.VMEM((10 * PLANE, CELLS), F32),
            pltpu.VMEM((4, 5 * PLANE, CELLS), F32),
            pltpu.VMEM((4, 5 * PLANE, CELLS), F32),
            pltpu.SemaphoreType.DMA((12,)),
            pltpu.SemaphoreType.DMA((4,)),
            pltpu.SemaphoreType.DMA((4,)),
        ],
        compiler_params=pltpu.CompilerParams(
            vmem_limit_bytes=VMEM_LIMIT, collective_id=0, has_side_effects=True
        ),
        name="step",
    )(in_hbm(solution), in_hbm(material), in_hbm(neighbours), refine_count, in_hbm(table))


def finish(nodal, middle):
    return pl.pallas_call(
        finish_kernel,
        out_shape=shape(9, CELLS, NODES),
        in_specs=[pl.BlockSpec(memory_space=pltpu.VMEM)] * 2,
        out_specs=pl.BlockSpec(memory_space=pltpu.MemorySpace.HBM),
        scratch_shapes=[pltpu.VMEM((18, CELLS, 128), F32), pltpu.SemaphoreType.DMA((27,))],
        compiler_params=pltpu.CompilerParams(vmem_limit_bytes=VMEM_LIMIT),
        name="finish",
    )(nodal, middle)


def on_device(solution, material, neighbours, refine_count):
    return finish(*step(solution, material, neighbours, refine_count))


def solution(mesh):
    in_specs = (
        P(None, ("space", "help"), None),
        P(None, ("space", "help"), None),
        P(None, ("space", "help")),
        P("space", "help"),
    )
    out_specs = P(None, ("space", "help"), None)
    return jax.shard_map(
        on_device, mesh=mesh, in_specs=in_specs, out_specs=out_specs, check_vma=False
    )
```
